256 devices in a mesh: rep: 16 (over y, x_hi, core), fsdp: 16 (over z, x_lo).
Axes of the slice: x: 4 (x_hi: 2, x_lo: 2; x = x_hi * 2 + x_lo), y: 4, z: 8, core: 2. Of those that a mesh axis runs over, the one named last changes fastest.
Arguments:
- activations: bfloat16 [16, 6144, 4096], P('rep', 'fsdp'), may hold values from -6 to 6
- kv_weight: bfloat16 [16, 4096, 1024], P('rep', 'fsdp'), may hold values from -0.09375 to 0.09375
- kv_cotangent: bfloat16 [16, 6144, 1024], P('rep', 'fsdp'), may hold values from -6 to 6
- first_moment: float32 [16, 4096, 1024], P('rep', 'fsdp'), may hold values from -48 to 48
- second_moment: float32 [16, 4096, 1024], P('rep', 'fsdp'), may hold values from 10 to 1000
- partner: int32 [16], replicated, may hold values from 0 to 15, as said below
- mix_numerator: int32 [16], replicated, may hold values from 8 to 56
Outputs:
- kv_out: bfloat16 [16, 6144, 1024], P('rep', 'fsdp')
- x_grad: bfloat16 [16, 6144, 4096], P('rep', 'fsdp')
- new_weight: bfloat16 [16, 4096, 1024], P('rep', 'fsdp')
- new_first: float32 [16, 4096, 1024], P('rep', 'fsdp')
- new_second: float32 [16, 4096, 1024], P('rep', 'fsdp')
The draws below stay inside these ranges and needn't reach their ends.
Inputs may be any that keep to these rules, and one draw needn't show every extreme that they name: partner[partner[r]] == r and partner[r] != r for every replica r.
All inputs are finite; a program needn't handle non-finite values.
Results may differ from the reference program's by a relative error of at most 0.018.
Values may be sent and summed in bfloat16 or wider, within the bound.
A program may use at most 128 MiB of HBM per device.

```python
import math
import jax
import jax.numpy as jnp
from jax import lax

D = 4096
KV2 = 1024
TOK_DEV = 384
TOKENS = 6144
N_REP = 16
N_FSDP = 16


def draw_partner(key, part):
    shuffled = jax.random.permutation(jax.random.fold_in(key, 7), N_REP).astype(jnp.int32)
    leading = shuffled[0::2]
    trailing = shuffled[1::2]
    matches = jnp.zeros((N_REP,), jnp.int32).at[leading].set(trailing).at[trailing].set(leading)
    return matches


def with_ends(entries, stream_key, low, largest):
    spot = [jax.random.randint(jax.random.fold_in(stream_key, axis), (), 0, length) for axis, length in enumerate(entries.shape)]
    main_axis = entries.shape.index(max(entries.shape))
    neighbour = spot[:main_axis] + [(spot[main_axis] + 1) % entries.shape[main_axis]] + spot[main_axis + 1:]
    return entries.at[tuple(spot)].set(low).at[tuple(neighbour)].set(largest)


def spiked(result, rng, source, target, parts, factor):
    owner, partner = [(jnp.arange(result.shape[position]) // (result.shape[position] // parts)).reshape([-1 if axis == position else 1 for axis in range(result.ndim)]) for position in (source, target)]
    chosen = jax.random.permutation(rng, parts)[partner]
    strong = (owner == chosen) | (owner == (partner + parts // 2) % parts)
    return jnp.where(strong, factor * result, result)


def shard_levels(own_key, dims, pieces, least, top_value):
    def one(dim, parts):
        heights = jax.random.uniform(jax.random.fold_in(jax.random.fold_in(own_key, 6), dim), (parts,), jnp.float32, least / len(pieces), top_value / len(pieces))
        return jnp.repeat(jnp.exp(heights), dims[dim] // parts).reshape((-1,) + (1,) * (len(dims) - dim - 1))

    loudness = one(*pieces[0])
    for cut in pieces[1:]:
        loudness = loudness * one(*cut)
    return loudness


def noise(stream_key, extent, spread, bound, split=(), kind=jnp.bfloat16):
    values = jax.random.normal(stream_key, extent, jnp.float32) * spread
    if len(split) > 0:
        values = shard_levels(stream_key, extent, split, -0.22, 0.18) * values
    return jnp.clip(values, min=-bound, max=bound).astype(kind)


def heavy_noise(own_key, dims, scale, bound, shards, heavy, dtype=jnp.bfloat16):
    values = scale * jax.random.normal(own_key, dims, jnp.float32)
    if shards:
        values = values * shard_levels(own_key, dims, shards, -0.22, 0.18)
    return jnp.clip(spiked(values, jax.random.fold_in(own_key, 3), *heavy), -bound, bound).astype(dtype)


def setup_inputs(seed: int = 0) -> dict:
    splits = jax.random.split(jax.random.key(seed), 8)
    return {
        "activations": heavy_noise(splits[0], (N_REP, TOKENS, D), 1.0, 6.0, ((0, 16), (1, 16)), (1, 2, 16, 2.0)),
        "kv_weight": noise(splits[1], (N_REP, D, KV2), D ** -0.5, 0.09375, ((0, 16), (1, 16))),
        "kv_cotangent": noise(splits[2], (N_REP, TOKENS, KV2), 1.0, 6.0, ((0, 16), (1, 16))),
        "first_moment": noise(splits[3], (N_REP, D, KV2), 8.0, 48.0, ((0, 16), (1, 16)), jnp.float32),
        "second_moment": jnp.clip(jnp.exp(math.log(1000.0) - 4.6051702 * jax.random.uniform(splits[4], (N_REP, D, KV2), jnp.float32) ** shard_levels(splits[4], (N_REP, D, KV2), ((0, 16), (1, 16)), -0.2, 0.2)), 10.0, 1000.0),
        "partner": draw_partner(jax.random.fold_in(splits[7], 71), 0),
        "mix_numerator": with_ends(jax.random.randint(splits[6], (N_REP,), 8, 57), jax.random.fold_in(splits[6], 1), 8, 56).astype(jnp.int32),
    }


beta_one = 0.9
beta_two = 0.999
learn_rate = 0.02
weight_decay = 0.1
adam_eps = 1e-08
corr_one = 1.0 - beta_one ** 10
corr_two = 1.0 - beta_two ** 10
mix_denom = 64.0

def reference(activations, kv_weight, kv_cotangent, first_moment, second_moment, partner, mix_numerator):

    def per_replica(inputs):
        tokens_in, weights, cotangent, moment_a, moment_b = inputs
        keys_values = jnp.dot(tokens_in, weights, preferred_element_type=jnp.float32).astype(jnp.bfloat16)
        input_grad = jnp.dot(cotangent, weights.T, preferred_element_type=jnp.float32).astype(jnp.bfloat16)
        token_groups = tokens_in.reshape(N_FSDP, TOK_DEV, D)
        cot_groups = cotangent.reshape(N_FSDP, TOK_DEV, KV2)

        def add_group(running, couple):
            partial_term = jnp.dot(couple[0].T, couple[1], preferred_element_type=jnp.float32).astype(jnp.bfloat16)
            partial_term = lax.optimization_barrier(partial_term)
            return (running + partial_term.astype(jnp.float32), None)
        gradient, _ = lax.scan(add_group, jnp.zeros((D, KV2), jnp.float32), (token_groups, cot_groups))
        moment_new_a = beta_one * moment_a + (1.0 - beta_one) * gradient
        moment_new_b = beta_two * moment_b + (1.0 - beta_two) * gradient * gradient
        old_weight = weights.astype(jnp.float32)
        update = moment_new_a / corr_one / (jnp.sqrt(moment_new_b / corr_two) + adam_eps) + weight_decay * old_weight
        stepped = (old_weight - learn_rate * update).astype(jnp.bfloat16)
        return (keys_values, input_grad, stepped, moment_new_a, moment_new_b)
    kv_out, x_grad, stepped, new_first, new_second = lax.map(per_replica, (activations, kv_weight, kv_cotangent, first_moment, second_moment))
    mixing = mix_numerator.astype(jnp.float32) / mix_denom
    partner_rows = jnp.take(stepped, partner.astype(jnp.int32), axis=0)
    new_weight = ((1.0 - mixing)[:, None, None] * stepped.astype(jnp.float32) + mixing[:, None, None] * partner_rows.astype(jnp.float32)).astype(jnp.bfloat16)
    return (kv_out, x_grad, new_weight, new_first, new_second)
```

```python
import functools

import jax
import jax.numpy as jnp
from jax import lax
from jax.experimental import pallas as pl
from jax.experimental.pallas import tpu as pltpu
from jax.sharding import PartitionSpec as P

beta_one = 0.9
beta_two = 0.999
learn_rate = 0.02
weight_decay = 0.1
adam_eps = 1e-08
corr_one = 1.0 - beta_one**10
corr_two = 1.0 - beta_two**10
mix_denom = 64.0

MESH = pl.DeviceIdType.MESH
BF = jnp.bfloat16
F32 = jnp.float32
NZ = 8
ORDER = (4, 3, 5, 2, 6, 1, 7, 0)
ROWS_X = 96


def kernel(
    act_h, w_h, cot_h, first_h, second_h, partner_s, mix_s,
    kv_h, xg_h, nw_h, nf_h, ns_h,
    acat, aoth, ccat, wg, kvacc, kvb, xgv, mom, mnew, rs_in, rs_out, gbuf,
    stepped, inbox, outbox, final, nwv,
    load_sem, act_sem, x_send, x_recv, wx_send, wx_recv, ag_send, ag_recv,
    rs_send, rs_recv, ex_send, ex_recv, out_sem, xg_sem,
):
    rep = lax.axis_index("rep")
    me = lax.axis_index("fsdp")
    n_rep = inbox.shape[0]
    tok = cot_h.shape[0]
    rows = w_h.shape[0]
    half = rows // 2
    z, xl = me // 2, me % 2
    up = (rep, lax.rem(z + 1, NZ) * 2 + xl)
    down = (rep, lax.rem(z + NZ - 1, NZ) * 2 + xl)
    side = (rep, z * 2 + 1 - xl)
    ring = (up, down)

    def block_columns(ref, col, slot):
        x = xl if col == 0 else 1 - xl
        index = lax.rem(z + slot, NZ) * 2 + x
        return ref.at[:, pl.ds(pl.multiple_of(index * rows, rows), rows)]

    def remote(src, dst, send, recv, target):
        return pltpu.make_async_remote_copy(
            src_ref=src, dst_ref=dst, send_sem=send, recv_sem=recv,
            device_id=target, device_id_type=MESH,
        )

    loads = {
        "cot": pltpu.make_async_copy(cot_h, ccat.at[pl.ds(0, tok)], load_sem.at[0]),
        "w": pltpu.make_async_copy(w_h, wg.at[0, 0], load_sem.at[1]),
        "first": pltpu.make_async_copy(first_h, mom.at[0], load_sem.at[2]),
        "second": pltpu.make_async_copy(second_h, mom.at[1], load_sem.at[3]),
    }
    for slot in range(NZ):
        loads[0, slot] = pltpu.make_async_copy(
            block_columns(act_h, 0, slot), acat.at[slot, pl.ds(0, tok)], act_sem.at[0, slot]
        )
        loads[1, slot] = pltpu.make_async_copy(
            block_columns(act_h, 1, slot), aoth.at[slot], act_sem.at[1, slot]
        )

    barrier = pltpu.get_barrier_semaphore()
    others = [(lax.rem(rep + k, n_rep), me) for k in range(1, n_rep)]
    for device in (up, down, side, *others):
        pl.semaphore_signal(barrier, inc=1, device_id=device, device_id_type=MESH)
    loads["cot"].start()
    loads["w"].start()
    for slot in (0, 7, 1, 4, 3, 5, 2, 6):
        loads[0, slot].start()
    pl.semaphore_wait(barrier, 3 + n_rep - 1)

    x_copies = {"cot": remote(cot_h, ccat.at[pl.ds(tok, tok)], x_send.at[NZ], x_recv.at[NZ], side)}
    for slot in ORDER:
        x_copies[slot] = remote(
            block_columns(act_h, 1, slot), acat.at[slot, pl.ds(tok, tok)],
            x_send.at[slot], x_recv.at[slot], side,
        )
    wx = [remote(w_h, wg.at[1, 0], wx_send.at[0], wx_recv.at[0], side)]
    for slot in range(1, NZ):
        wx.append(
            remote(
                wg.at[0, slot, pl.ds(0, ROWS_X)], wg.at[1, slot, pl.ds(0, ROWS_X)],
                wx_send.at[slot], wx_recv.at[slot], side,
            )
        )

    def gather(col, direction, hop):
        low, high = (0, rows) if col == 0 else (ROWS_X, rows)
        if hop == NZ // 2:
            middle = (low + high) // 2
            low, high = (low, middle) if direction == 0 else (middle, high)
        if direction == 0:
            src, dst = (NZ - hop + 1) % NZ, NZ - hop
        else:
            src, dst = hop - 1, hop
        span = pl.ds(low, high - low)
        source = w_h.at[span] if (col == 0 and hop == 1) else wg.at[col, src, span]
        return remote(
            source, wg.at[col, dst, span],
            ag_send.at[col, direction, hop - 1], ag_recv.at[col, direction, hop - 1],
            ring[direction],
        )

    ag = {
        (c, d, h): gather(c, d, h) for c in range(2) for d in range(2) for h in range(1, NZ // 2 + 1)
    }

    def gather_start(col, hop):
        for direction in range(2):
            ag[col, direction, hop].start()

    def gather_arrived(col, hop):
        for direction in range(2):
            ag[col, direction, hop].wait_recv()

    xg_copies = []

    def use_block(col, slot, first=False):
        block = wg[col, slot]
        tokens = acat[slot, pl.ds(0, tok)] if col == 0 else aoth[slot]
        term = jnp.dot(tokens, block, preferred_element_type=F32)
        if first:
            kvacc[...] = term
        else:
            kvacc[...] += term
        xgv[col, slot] = lax.dot_general(
            ccat[pl.ds(0, tok)], block, (((1,), (1,)), ((), ())), preferred_element_type=F32
        ).astype(BF)
        copy = pltpu.make_async_copy(
            xgv.at[col, slot], block_columns(xg_h, col, slot), xg_sem.at[col, slot]
        )
        copy.start()
        xg_copies.append(copy)

    def product(slot):
        return lax.dot_general(
            acat[slot], ccat[...], (((0,), (0,)), ((), ())), preferred_element_type=F32
        )

    def reduce_copy(direction, step, part):
        span = pl.ds(part * half, half)
        return remote(
            rs_out.at[direction, step, span], rs_in.at[direction, step, span],
            rs_send.at[direction, step, part], rs_recv.at[direction, step, part],
            ring[direction],
        )

    rs = {(0, 0, 0): reduce_copy(0, 0, 0), (1, 0, 1): reduce_copy(1, 0, 1)}
    for direction in range(2):
        for step in range(1, NZ // 2):
            for part in range(2):
                rs[direction, step, part] = reduce_copy(direction, step, part)

    def reduce_step(step):
        slots = (NZ // 2 - step, NZ // 2 + step)
        for direction in range(2):
            x_copies[slots[direction]].wait_recv()
            gbuf[direction] = product(slots[direction])
        for part in range(2):
            for direction in range(2):
                p = part if step > 1 else (1 - part if direction == 0 else part)
                span = pl.ds(p * half, half)
                value = gbuf[direction, span]
                if (direction, step - 1, p) in rs:
                    rs[direction, step - 1, p].wait_recv()
                    value = value + rs_in[direction, step - 1, span].astype(F32)
                rs_out[direction, step, span] = value.astype(BF)
                rs[direction, step, p].start()

    x_copies["cot"].start()
    gather_start(0, 1)
    for slot in ORDER:
        x_copies[slot].start()
    wx[0].start()
    for slot in range(NZ):
        loads[1, slot].start()
    loads["first"].start()
    loads["second"].start()

    loads["cot"].wait()
    loads["w"].wait()
    for slot in range(NZ):
        loads[0, slot].wait()
    use_block(0, 0, first=True)
    gather_arrived(0, 1)
    gather_start(0, 2)
    wx[7].start()
    wx[1].start()
    use_block(0, 7)
    use_block(0, 1)

    x_copies["cot"].wait_recv()
    x_copies[4].wait_recv()
    gbuf[0] = product(4)
    rs_out[0, 0, pl.ds(0, half)] = gbuf[0, pl.ds(0, half)].astype(BF)
    rs[0, 0, 0].start()
    rs_out[1, 0, pl.ds(half, half)] = gbuf[0, pl.ds(half, half)].astype(BF)
    rs[1, 0, 1].start()

    gather_arrived(0, 2)
    gather_start(0, 3)
    wx[6].start()
    wx[2].start()
    use_block(0, 6)
    use_block(0, 2)

    reduce_step(1)
    reduce_step(2)
    gather_arrived(0, 3)
    gather_start(0, 4)
    wx[5].start()
    wx[3].start()
    reduce_step(3)
    use_block(0, 5)
    use_block(0, 3)
    x_copies[0].wait_recv()
    gbuf[0] = product(0)
    wx[0].wait_recv()
    gather_start(1, 1)
    loads["first"].wait()
    loads["second"].wait()
    for part in range(2):
        span = pl.ds(part * half, half)
        for direction in range(2):
            rs[direction, NZ // 2 - 1, part].wait_recv()
        grad = (
            gbuf[0, span]
            + rs_in[0, NZ // 2 - 1, span].astype(F32)
            + rs_in[1, NZ // 2 - 1, span].astype(F32)
        )
        new_a = beta_one * mom[0, span] + (1.0 - beta_one) * grad
        new_b = beta_two * mom[1, span] + (1.0 - beta_two) * grad * grad
        mnew[0, span] = new_a
        mnew[1, span] = new_b
        old = wg[0, 0, span].astype(F32)
        update = new_a / corr_one / (jnp.sqrt(new_b / corr_two) + adam_eps) + weight_decay * old
        count = n_rep // 2
        stepped[pl.ds(part * count, count)] = (
            (old - learn_rate * update).astype(BF).reshape(count, half // count, old.shape[1])
        )
    outs = [
        pltpu.make_async_copy(mnew.at[0], nf_h, out_sem.at[0]),
        pltpu.make_async_copy(mnew.at[1], ns_h, out_sem.at[1]),
    ]
    for copy in outs:
        copy.start()

    def exchange(phase, k):
        peer = lax.rem(rep + k, n_rep)
        src = (stepped if phase == 0 else outbox).at[peer]
        dst = (inbox if phase == 0 else final).at[rep]
        return remote(src, dst, ex_send.at[phase, k], ex_recv.at[phase, k], (peer, me))

    ex = [[exchange(phase, k) for k in range(1, n_rep)] for phase in range(2)]
    for copy in ex[0]:
        copy.start()
    inbox[rep] = stepped[rep]

    gather_arrived(0, 4)
    wx[4].start()
    gather_arrived(1, 1)
    gather_start(1, 2)
    for copy in ex[0]:
        copy.wait_recv()
    for j in range(n_rep):
        outbox[j] = inbox[partner_s[j]]
    for copy in ex[1]:
        copy.start()
    final[rep] = outbox[rep]

    for slot in range(NZ):
        loads[1, slot].wait()
    use_block(0, 4)
    use_block(1, 0)
    gather_arrived(1, 2)
    gather_start(1, 3)
    for slot in (7, 1, 6, 2):
        wx[slot].wait_recv()
        use_block(1, slot)
    for copy in ex[1]:
        copy.wait_recv()
    mixing = mix_s[rep].astype(F32) / mix_denom
    nwv[...] = (
        (1.0 - mixing) * stepped[...].astype(F32) + mixing * final[...].astype(F32)
    ).astype(BF).reshape(nwv.shape)
    copy = pltpu.make_async_copy(nwv, nw_h, out_sem.at[2])
    copy.start()
    outs.append(copy)
    gather_arrived(1, 3)
    gather_start(1, 4)
    for slot in (5, 3):
        wx[slot].wait_recv()
        use_block(1, slot)
    gather_arrived(1, 4)
    wx[4].wait_recv()
    use_block(1, 4)
    kvb[...] = kvacc[...].astype(BF)
    copy = pltpu.make_async_copy(kvb, kv_h, out_sem.at[3])
    copy.start()
    outs.append(copy)

    for copy in (*x_copies.values(), *wx, *ag.values(), *rs.values(), *ex[0], *ex[1]):
        copy.wait_send()
    for copy in (*outs, *xg_copies):
        copy.wait()


def per_device(
    activations, kv_weight, kv_cotangent, first_moment, second_moment, partner, mix_numerator
):
    act, weights, cot = activations[0], kv_weight[0], kv_cotangent[0]
    tok, width = act.shape
    rows, cols = weights.shape
    n_rep = partner.shape[0]
    dma = pltpu.SemaphoreType.DMA
    hops = NZ // 2
    hbm = pl.BlockSpec(memory_space=pl.ANY)
    smem = pl.BlockSpec(memory_space=pltpu.SMEM)
    outs = pl.pallas_call(
        kernel,
        out_shape=(
            jax.ShapeDtypeStruct((tok, cols), BF),
            jax.ShapeDtypeStruct((tok, width), BF),
            jax.ShapeDtypeStruct((rows, cols), BF),
            jax.ShapeDtypeStruct((rows, cols), F32),
            jax.ShapeDtypeStruct((rows, cols), F32),
        ),
        in_specs=[hbm] * 5 + [smem] * 2,
        out_specs=[hbm] * 5,
        scratch_shapes=[
            pltpu.VMEM((NZ, 2 * tok, rows), BF),
            pltpu.VMEM((NZ, tok, rows), BF),
            pltpu.VMEM((2 * tok, cols), BF),
            pltpu.VMEM((2, NZ, rows, cols), BF),
            pltpu.VMEM((tok, cols), F32),
            pltpu.VMEM((tok, cols), BF),
            pltpu.VMEM((2, NZ, tok, rows), BF),
            pltpu.VMEM((2, rows, cols), F32),
            pltpu.VMEM((2, rows, cols), F32),
            pltpu.VMEM((2, hops, rows, cols), BF),
            pltpu.VMEM((2, hops, rows, cols), BF),
            pltpu.VMEM((2, rows, cols), F32),
            pltpu.VMEM((n_rep, rows // n_rep, cols), BF),
            pltpu.VMEM((n_rep, rows // n_rep, cols), BF),
            pltpu.VMEM((n_rep, rows // n_rep, cols), BF),
            pltpu.VMEM((n_rep, rows // n_rep, cols), BF),
            pltpu.VMEM((rows, cols), BF),
            dma((4,)),
            dma((2, NZ)),
            dma((NZ + 1,)),
            dma((NZ + 1,)),
            dma((NZ,)),
            dma((NZ,)),
            dma((2, 2, hops)),
            dma((2, 2, hops)),
            dma((2, hops, 2)),
            dma((2, hops, 2)),
            dma((2, n_rep)),
            dma((2, n_rep)),
            dma((4,)),
            dma((2, NZ)),
        ],
        name="step",
        compiler_params=pltpu.CompilerParams(
            collective_id=0, has_side_effects=True, vmem_limit_bytes=52 << 20
        ),
    )(act, weights, cot, first_moment[0], second_moment[0], partner, mix_numerator)
    return tuple(out[None] for out in outs)


def solution(mesh):
    split = P("rep", "fsdp", None)
    return jax.shard_map(
        per_device,
        mesh=mesh,
        in_specs=(split,) * 5 + (P(), P()),
        out_specs=(split,) * 5,
        check_vma=False,
    )
```

```python
import functools

import jax
import jax.numpy as jnp
from jax import lax
from jax.experimental import pallas as pl
from jax.experimental.pallas import tpu as pltpu
from jax.sharding import PartitionSpec as P

beta_one = 0.9
beta_two = 0.999
learn_rate = 0.02
weight_decay = 0.1
adam_eps = 1e-08
corr_one = 1.0 - beta_one**10
corr_two = 1.0 - beta_two**10
mix_denom = 64.0

MESH = pl.DeviceIdType.MESH
BF = jnp.bfloat16
F32 = jnp.float32
NZ = 8
ORDER = (4, 3, 5, 2, 6, 1, 7, 0)
ROWS_X = 96


def kernel(
    act_h, w_h, cot_h, first_h, second_h, partner_h, mix_h,
    kvb, xgv, nwv, first_new, second_new,
    acat, aoth, ccat, wg, kvacc, mom, rs_in, rs_out, gbuf,
    stepped, inbox, outbox, final, scalars,
    load_sem, act_sem, x_send, x_recv, wx_send, wx_recv, ag_send, ag_recv,
    rs_send, rs_recv, ex_send, ex_recv,
):
    rep = lax.axis_index("rep")
    me = lax.axis_index("fsdp")
    n_rep = inbox.shape[0]
    tok = cot_h.shape[0]
    rows = w_h.shape[0]
    half = rows // 2
    z, xl = me // 2, me % 2
    up = (rep, lax.rem(z + 1, NZ) * 2 + xl)
    down = (rep, lax.rem(z + NZ - 1, NZ) * 2 + xl)
    side = (rep, z * 2 + 1 - xl)
    ring = (up, down)

    def block_columns(ref, col, slot):
        x = xl if col == 0 else 1 - xl
        index = lax.rem(z + slot, NZ) * 2 + x
        return ref.at[:, pl.ds(pl.multiple_of(index * rows, rows), rows)]

    def remote(src, dst, send, recv, target):
        return pltpu.make_async_remote_copy(
            src_ref=src, dst_ref=dst, send_sem=send, recv_sem=recv,
            device_id=target, device_id_type=MESH,
        )

    loads = {
        "cot": pltpu.make_async_copy(cot_h, ccat.at[pl.ds(0, tok)], load_sem.at[0]),
        "w": pltpu.make_async_copy(w_h, wg.at[0, 0], load_sem.at[1]),
        "first": pltpu.make_async_copy(first_h, mom.at[0], load_sem.at[2]),
        "second": pltpu.make_async_copy(second_h, mom.at[1], load_sem.at[3]),
        "partner": pltpu.make_async_copy(partner_h, scalars.at[0], load_sem.at[4]),
        "mix": pltpu.make_async_copy(mix_h, scalars.at[1], load_sem.at[5]),
    }
    for slot in range(NZ):
        loads[0, slot] = pltpu.make_async_copy(
            block_columns(act_h, 0, slot), acat.at[slot, pl.ds(0, tok)], act_sem.at[0, slot]
        )
        loads[1, slot] = pltpu.make_async_copy(
            block_columns(act_h, 1, slot), aoth.at[slot], act_sem.at[1, slot]
        )

    barrier = pltpu.get_barrier_semaphore()
    others = [(lax.rem(rep + k, n_rep), me) for k in range(1, n_rep)]
    for device in (up, down, side, *others):
        pl.semaphore_signal(barrier, inc=1, device_id=device, device_id_type=MESH)
    loads["cot"].start()
    loads["w"].start()
    for slot in (0, 7, 1, 4, 3, 5, 2, 6):
        loads[0, slot].start()
    pl.semaphore_wait(barrier, 3 + n_rep - 1)

    x_copies = {"cot": remote(cot_h, ccat.at[pl.ds(tok, tok)], x_send.at[NZ], x_recv.at[NZ], side)}
    for slot in ORDER:
        x_copies[slot] = remote(
            block_columns(act_h, 1, slot), acat.at[slot, pl.ds(tok, tok)],
            x_send.at[slot], x_recv.at[slot], side,
        )
    wx = [remote(w_h, wg.at[1, 0], wx_send.at[0], wx_recv.at[0], side)]
    for slot in range(1, NZ):
        wx.append(
            remote(
                wg.at[0, slot, pl.ds(0, ROWS_X)], wg.at[1, slot, pl.ds(0, ROWS_X)],
                wx_send.at[slot], wx_recv.at[slot], side,
            )
        )

    def gather(col, direction, hop):
        low, high = (0, rows) if col == 0 else (ROWS_X, rows)
        if hop == NZ // 2:
            middle = (low + high) // 2
            low, high = (low, middle) if direction == 0 else (middle, high)
        if direction == 0:
            src, dst = (NZ - hop + 1) % NZ, NZ - hop
        else:
            src, dst = hop - 1, hop
        span = pl.ds(low, high - low)
        source = w_h.at[span] if (col == 0 and hop == 1) else wg.at[col, src, span]
        return remote(
            source, wg.at[col, dst, span],
            ag_send.at[col, direction, hop - 1], ag_recv.at[col, direction, hop - 1],
            ring[direction],
        )

    ag = {
        (c, d, h): gather(c, d, h) for c in range(2) for d in range(2) for h in range(1, NZ // 2 + 1)
    }

    def gather_start(col, hop):
        for direction in range(2):
            ag[col, direction, hop].start()

    def gather_arrived(col, hop):
        for direction in range(2):
            ag[col, direction, hop].wait_recv()

    def use_block(col, slot, first=False):
        block = wg[col, slot]
        tokens = acat[slot, pl.ds(0, tok)] if col == 0 else aoth[slot]
        term = jnp.dot(tokens, block, preferred_element_type=F32)
        if first:
            kvacc[...] = term
        else:
            kvacc[...] += term
        x = xl if col == 0 else 1 - xl
        xgv[lax.rem(z + slot, NZ) * 2 + x] = lax.dot_general(
            ccat[pl.ds(0, tok)], block, (((1,), (1,)), ((), ())), preferred_element_type=F32
        ).astype(BF)

    def product(slot):
        return lax.dot_general(
            acat[slot], ccat[...], (((0,), (0,)), ((), ())), preferred_element_type=F32
        )

    def reduce_copy(direction, step, part):
        span = pl.ds(part * half, half)
        return remote(
            rs_out.at[direction, step, span], rs_in.at[direction, step, span],
            rs_send.at[direction, step, part], rs_recv.at[direction, step, part],
            ring[direction],
        )

    rs = {(0, 0, 0): reduce_copy(0, 0, 0), (1, 0, 1): reduce_copy(1, 0, 1)}
    for direction in range(2):
        for step in range(1, NZ // 2):
            for part in range(2):
                rs[direction, step, part] = reduce_copy(direction, step, part)

    def reduce_step(step):
        slots = (NZ // 2 - step, NZ // 2 + step)
        for direction in range(2):
            x_copies[slots[direction]].wait_recv()
            gbuf[direction] = product(slots[direction])
        for part in range(2):
            for direction in range(2):
                p = part if step > 1 else (1 - part if direction == 0 else part)
                span = pl.ds(p * half, half)
                value = gbuf[direction, span]
                if (direction, step - 1, p) in rs:
                    rs[direction, step - 1, p].wait_recv()
                    value = value + rs_in[direction, step - 1, span].astype(F32)
                rs_out[direction, step, span] = value.astype(BF)
                rs[direction, step, p].start()

    x_copies["cot"].start()
    gather_start(0, 1)
    for slot in ORDER:
        x_copies[slot].start()
    wx[0].start()
    for slot in range(NZ):
        loads[1, slot].start()
    for name in ("first", "second", "partner", "mix"):
        loads[name].start()

    loads["cot"].wait()
    loads["w"].wait()
    for slot in range(NZ):
        loads[0, slot].wait()
    use_block(0, 0, first=True)
    gather_arrived(0, 1)
    gather_start(0, 2)
    wx[7].start()
    wx[1].start()
    use_block(0, 7)
    use_block(0, 1)

    x_copies["cot"].wait_recv()
    x_copies[4].wait_recv()
    gbuf[0] = product(4)
    rs_out[0, 0, pl.ds(0, half)] = gbuf[0, pl.ds(0, half)].astype(BF)
    rs[0, 0, 0].start()
    rs_out[1, 0, pl.ds(half, half)] = gbuf[0, pl.ds(half, half)].astype(BF)
    rs[1, 0, 1].start()

    gather_arrived(0, 2)
    gather_start(0, 3)
    wx[6].start()
    wx[2].start()
    use_block(0, 6)
    use_block(0, 2)

    reduce_step(1)
    reduce_step(2)
    gather_arrived(0, 3)
    gather_start(0, 4)
    wx[5].start()
    wx[3].start()
    reduce_step(3)
    use_block(0, 5)
    use_block(0, 3)
    x_copies[0].wait_recv()
    gbuf[0] = product(0)
    wx[0].wait_recv()
    gather_start(1, 1)
    loads["first"].wait()
    loads["second"].wait()
    for part in range(2):
        span = pl.ds(part * half, half)
        for direction in range(2):
            rs[direction, NZ // 2 - 1, part].wait_recv()
        grad = (
            gbuf[0, span]
            + rs_in[0, NZ // 2 - 1, span].astype(F32)
            + rs_in[1, NZ // 2 - 1, span].astype(F32)
        )
        new_a = beta_one * mom[0, span] + (1.0 - beta_one) * grad
        new_b = beta_two * mom[1, span] + (1.0 - beta_two) * grad * grad
        first_new[span] = new_a
        second_new[span] = new_b
        old = wg[0, 0, span].astype(F32)
        update = new_a / corr_one / (jnp.sqrt(new_b / corr_two) + adam_eps) + weight_decay * old
        count = n_rep // 2
        stepped[pl.ds(part * count, count)] = (
            (old - learn_rate * update).astype(BF).reshape(count, half // count, old.shape[1])
        )
    def exchange(phase, k):
        peer = lax.rem(rep + k, n_rep)
        src = (stepped if phase == 0 else outbox).at[peer]
        dst = (inbox if phase == 0 else final).at[rep]
        return remote(src, dst, ex_send.at[phase, k], ex_recv.at[phase, k], (peer, me))

    ex = [[exchange(phase, k) for k in range(1, n_rep)] for phase in range(2)]
    for copy in ex[0]:
        copy.start()
    inbox[rep] = stepped[rep]

    gather_arrived(0, 4)
    wx[4].start()
    gather_arrived(1, 1)
    gather_start(1, 2)
    for copy in ex[0]:
        copy.wait_recv()
    loads["partner"].wait()
    loads["mix"].wait()
    for j in range(n_rep):
        outbox[j] = inbox[scalars[0, j]]
    for copy in ex[1]:
        copy.start()
    final[rep] = outbox[rep]

    for slot in range(NZ):
        loads[1, slot].wait()
    use_block(0, 4)
    use_block(1, 0)
    gather_arrived(1, 2)
    gather_start(1, 3)
    for slot in (7, 1, 6, 2):
        wx[slot].wait_recv()
        use_block(1, slot)
    for copy in ex[1]:
        copy.wait_recv()
    mixing = scalars[1, rep].astype(F32) / mix_denom
    nwv[...] = (
        (1.0 - mixing) * stepped[...].astype(F32) + mixing * final[...].astype(F32)
    ).astype(BF).reshape(nwv.shape)
    gather_arrived(1, 3)
    gather_start(1, 4)
    for slot in (5, 3):
        wx[slot].wait_recv()
        use_block(1, slot)
    gather_arrived(1, 4)
    wx[4].wait_recv()
    use_block(1, 4)
    kvb[...] = kvacc[...].astype(BF)

    for copy in (*x_copies.values(), *wx, *ag.values(), *rs.values(), *ex[0], *ex[1]):
        copy.wait_send()


def write_out(kvb, xgv, nwv, first_new, second_new, kv_h, xg_h, nw_h, nf_h, ns_h, sem):
    rows = xgv.shape[2]
    pairs = [(xgv.at[i], xg_h.at[:, pl.ds(i * rows, rows)]) for i in range(xgv.shape[0])]
    pairs += [(kvb, kv_h), (nwv, nw_h), (first_new, nf_h), (second_new, ns_h)]
    copies = [pltpu.make_async_copy(a, b, sem.at[i]) for i, (a, b) in enumerate(pairs)]
    for copy in copies:
        copy.start()
    for copy in copies:
        copy.wait()


def per_device(
    activations, kv_weight, kv_cotangent, first_moment, second_moment, partner, mix_numerator
):
    act, weights, cot = activations[0], kv_weight[0], kv_cotangent[0]
    tok, width = act.shape
    rows, cols = weights.shape
    n_rep = partner.shape[0]
    dma = pltpu.SemaphoreType.DMA
    hops = NZ // 2
    hbm = pl.BlockSpec(memory_space=pltpu.HBM)
    vmem = pl.BlockSpec(memory_space=pltpu.VMEM)
    outs = pl.pallas_call(
        kernel,
        out_shape=(
            pltpu.VMEM((tok, cols), BF),
            pltpu.VMEM((width // rows, tok, rows), BF),
            pltpu.VMEM((rows, cols), BF),
            pltpu.VMEM((rows, cols), F32),
            pltpu.VMEM((rows, cols), F32),
        ),
        in_specs=[hbm] * 7,
        out_specs=[vmem] * 5,
        scratch_shapes=[
            pltpu.VMEM((NZ, 2 * tok, rows), BF),
            pltpu.VMEM((NZ, tok, rows), BF),
            pltpu.VMEM((2 * tok, cols), BF),
            pltpu.VMEM((2, NZ, rows, cols), BF),
            pltpu.VMEM((tok, cols), F32),
            pltpu.VMEM((2, rows, cols), F32),
            pltpu.VMEM((2, hops, rows, cols), BF),
            pltpu.VMEM((2, hops, rows, cols), BF),
            pltpu.VMEM((2, rows, cols), F32),
            pltpu.VMEM((n_rep, rows // n_rep, cols), BF),
            pltpu.VMEM((n_rep, rows // n_rep, cols), BF),
            pltpu.VMEM((n_rep, rows // n_rep, cols), BF),
            pltpu.VMEM((n_rep, rows // n_rep, cols), BF),
            pltpu.SMEM((2, n_rep), jnp.int32),
            dma((6,)),
            dma((2, NZ)),
            dma((NZ + 1,)),
            dma((NZ + 1,)),
            dma((NZ,)),
            dma((NZ,)),
            dma((2, 2, hops)),
            dma((2, 2, hops)),
            dma((2, hops, 2)),
            dma((2, hops, 2)),
            dma((2, n_rep)),
            dma((2, n_rep)),
        ],
        name="step",
        compiler_params=pltpu.CompilerParams(
            collective_id=0, has_side_effects=True, vmem_limit_bytes=44 << 20
        ),
    )(
        *(
            pltpu.with_memory_space_constraint(x, pltpu.HBM)
            for x in (act, weights, cot, first_moment[0], second_moment[0], partner, mix_numerator)
        )
    )
    outs = pl.pallas_call(
        write_out,
        out_shape=(
            jax.ShapeDtypeStruct((tok, cols), BF),
            jax.ShapeDtypeStruct((tok, width), BF),
            jax.ShapeDtypeStruct((rows, cols), BF),
            jax.ShapeDtypeStruct((rows, cols), F32),
            jax.ShapeDtypeStruct((rows, cols), F32),
        ),
        in_specs=[vmem] * 5,
        out_specs=[hbm] * 5,
        scratch_shapes=[dma((width // rows + 4,))],
        name="write_out",
        compiler_params=pltpu.CompilerParams(vmem_limit_bytes=1 << 20),
    )(*outs)
    return tuple(out[None] for out in outs)


def solution(mesh):
    split = P("rep", "fsdp", None)
    return jax.shard_map(
        per_device,
        mesh=mesh,
        in_specs=(split,) * 5 + (P(), P()),
        out_specs=(split,) * 5,
        check_vma=False,
    )
```

```python
import jax
import jax.numpy as jnp
from jax import lax
from jax.experimental import pallas as pl
from jax.experimental.pallas import tpu as pltpu
from jax.sharding import PartitionSpec as P

beta_one = 0.9
beta_two = 0.999
learn_rate = 0.02
weight_decay = 0.1
adam_eps = 1e-08
corr_one = 1.0 - beta_one**10
corr_two = 1.0 - beta_two**10
mix_denom = 64.0

MESH = pl.DeviceIdType.MESH
BF = jnp.bfloat16
F32 = jnp.float32
NZ = 8
HOPS = NZ // 2
ROWS_X = 96

SCHEDULE = (
    ("xs", 4), ("ag", 0, 0, 1), ("ag", 0, 1, 1), ("xs", "cot"), ("ag", 0, 0, 2), ("ag", 0, 1, 2),
    ("xs", 5), ("xs", 3), ("xs", 6), ("g", 4), ("rs", 1, 0, 1), ("rs", 0, 0, 0), ("g", 5),
    ("rs", 1, 1, 0), ("ag", 0, 0, 3), ("ag", 0, 1, 3), ("xs", 7), ("use", 0, 6), ("g", 6),
    ("xs", 2), ("use", 0, 1), ("wxB",), ("g", 3), ("rs", 0, 1, 0), ("rs", 0, 1, 1),
    ("rs", 1, 1, 1), ("xs", 1), ("use", 0, 7), ("ag", 1, 0, 1), ("wxA",), ("g", 2),
    ("ag", 1, 1, 1), ("g", 1), ("rs", 1, 2, 0), ("rs", 1, 2, 1), ("rs", 0, 2, 0), ("xs", 0),
    ("use", 1, 0), ("wx", 6), ("wx", 2), ("rs", 0, 2, 1), ("g", 7), ("rs", 0, 3, 0), ("wx", 7),
    ("rs", 1, 3, 0), ("rs", 1, 3, 1), ("ag", 1, 0, 2), ("g", 0), ("ag", 1, 1, 2), ("wx", 1),
    ("wx", 5), ("use", 1, 7), ("fin", 0), ("rs", 0, 3, 1), ("use", 0, 2), ("ex0", 0), ("wx", 3),
    ("ag", 0, 1, 4), ("ag", 0, 0, 4), ("ag", 1, 0, 3), ("use", 0, 5), ("ex1", 0), ("fin", 1),
    ("ex0", 1), ("ag", 1, 1, 3), ("use", 1, 1), ("use", 0, 0), ("use", 1, 2), ("ex1", 1),
    ("wx", 4), ("use", 0, 3), ("ag", 1, 0, 4), ("ag", 1, 1, 4), ("use", 1, 6), ("use", 0, 4),
)


def column_index(col, slot):
    me = lax.axis_index("fsdp")
    x = me % 2
    return lax.rem(me // 2 + slot, NZ) * 2 + (x if col == 0 else 1 - x)


def columns_of(ref, col, slot, rows):
    start = column_index(col, slot) * rows
    return ref.at[:, pl.ds(pl.multiple_of(start, rows), rows)]


def back_product(cot, block):
    return lax.dot_general(
        cot, block, (((1,), (1,)), ((), ())), preferred_element_type=F32
    ).astype(BF)


def kernel(
    act_h, w_h, cot_h, first_h, second_h, partner_h,
    kvacc, xgv, first_new, second_new, stepped, final, wg, aoth, ccat,
    acat, mom, rs_in, rs_out, gbuf, inbox_a, inbox_b, outbox, partner_s,
    load_sem, act_sem, x_send, x_recv, wx_send, wx_recv, ag_send, ag_recv,
    rs_send, rs_recv, ex_send, ex_recv,
):
    rep = lax.axis_index("rep")
    me = lax.axis_index("fsdp")
    inbox = (inbox_a, inbox_b)
    n_rep = inbox_a.shape[0]
    tok = cot_h.shape[0]
    rows, cols = w_h.shape
    half = cols // 2
    z, xl = me // 2, me % 2
    up = (rep, lax.rem(z + 1, NZ) * 2 + xl)
    down = (rep, lax.rem(z + NZ - 1, NZ) * 2 + xl)
    side = (rep, z * 2 + 1 - xl)
    ring = (up, down)

    def remote(src, dst, send, recv, target):
        return pltpu.make_async_remote_copy(
            src_ref=src, dst_ref=dst, send_sem=send, recv_sem=recv,
            device_id=target, device_id_type=MESH,
        )

    loads = {
        "cot": pltpu.make_async_copy(cot_h, ccat.at[pl.ds(0, tok)], load_sem.at[0]),
        "w": pltpu.make_async_copy(w_h, wg.at[0, 0], load_sem.at[1]),
        "first": pltpu.make_async_copy(first_h, mom.at[0], load_sem.at[2]),
        "second": pltpu.make_async_copy(second_h, mom.at[1], load_sem.at[3]),
        "partner": pltpu.make_async_copy(partner_h, partner_s, load_sem.at[4]),
    }
    for slot in range(NZ):
        loads[0, slot] = pltpu.make_async_copy(
            columns_of(act_h, 0, slot, rows), acat.at[slot, pl.ds(0, tok)], act_sem.at[0, slot]
        )
        loads[1, slot] = pltpu.make_async_copy(
            columns_of(act_h, 1, slot, rows), aoth.at[slot], act_sem.at[1, slot]
        )
    waited = set()

    def loaded(key):
        if key not in waited:
            waited.add(key)
            loads[key].wait()

    copies = {
        ("xs", "cot"): remote(
            cot_h, ccat.at[pl.ds(tok, tok)], x_send.at[NZ], x_recv.at[NZ], side
        ),
        ("wxA",): remote(
            w_h.at[pl.ds(0, ROWS_X)], wg.at[1, 0, pl.ds(0, ROWS_X)],
            wx_send.at[0], wx_recv.at[0], side,
        ),
        ("wxB",): remote(
            w_h.at[pl.ds(ROWS_X, rows - ROWS_X)], wg.at[1, 0, pl.ds(ROWS_X, rows - ROWS_X)],
            wx_send.at[NZ], wx_recv.at[NZ], side,
        ),
    }
    for slot in range(NZ):
        copies["xs", slot] = remote(
            columns_of(act_h, 1, slot, rows), acat.at[slot, pl.ds(tok, tok)],
            x_send.at[slot], x_recv.at[slot], side,
        )
        if slot > 0:
            copies["wx", slot] = remote(
                wg.at[0, slot, pl.ds(0, ROWS_X)], wg.at[1, slot, pl.ds(0, ROWS_X)],
                wx_send.at[slot], wx_recv.at[slot], side,
            )

    def gather(col, direction, hop):
        low, high = (0, rows) if col == 0 else (ROWS_X, rows)
        if hop == HOPS:
            middle = (low + high) // 2
            low, high = (low, middle) if direction == 0 else (middle, high)
        if direction == 0:
            src, dst = (NZ - hop + 1) % NZ, NZ - hop
        else:
            src, dst = hop - 1, hop
        span = pl.ds(low, high - low)
        source = w_h.at[span] if (col == 0 and hop == 1) else wg.at[col, src, span]
        return remote(
            source, wg.at[col, dst, span],
            ag_send.at[col, direction, hop - 1], ag_recv.at[col, direction, hop - 1],
            ring[direction],
        )

    def reduce_copy(direction, step, part):
        span = (direction, step, slice(None), pl.ds(part * half, half))
        return remote(
            rs_out.at[span], rs_in.at[span],
            rs_send.at[direction, step, part], rs_recv.at[direction, step, part],
            ring[direction],
        )

    for direction in range(2):
        for hop in range(1, HOPS + 1):
            for col in range(2):
                copies["ag", col, direction, hop] = gather(col, direction, hop)
        for step in range(HOPS):
            for part in range(2):
                if step > 0 or part == direction:
                    copies["rs", direction, step, part] = reduce_copy(direction, step, part)

    def exchange(phase, part):
        out = []
        for k in range(1, n_rep):
            peer = lax.rem(rep + k, n_rep)
            src = (stepped, outbox)[phase].at[part, peer]
            dst = final.at[part, rep] if phase else inbox[part].at[rep]
            out.append(
                remote(
                    src, dst,
                    ex_send.at[phase, part, k], ex_recv.at[phase, part, k], (peer, me),
                )
            )
        return out

    ex = {(phase, part): exchange(phase, part) for phase in range(2) for part in range(2)}

    def arrived(key):
        if key not in waited:
            waited.add(key)
            copies[key].wait_recv()

    def block_arrived(col, slot):
        if slot == 0:
            if col == 1:
                arrived(("wxB",))
        elif slot == HOPS:
            arrived(("ag", col, 0, HOPS))
            arrived(("ag", col, 1, HOPS))
        elif slot > HOPS:
            arrived(("ag", col, 0, NZ - slot))
        else:
            arrived(("ag", col, 1, slot))

    used = []

    def use_block(col, slot):
        block_arrived(col, slot)
        if col == 1:
            arrived(("wx", slot) if slot else ("wxA",))
        elif slot == 0:
            loaded("w")
        loaded("cot")
        loaded((col, slot))
        block = wg[col, slot]
        tokens = acat[slot, pl.ds(0, tok)] if col == 0 else aoth[slot]
        term = jnp.dot(tokens, block, preferred_element_type=F32)
        if used:
            kvacc[...] += term
        else:
            kvacc[...] = term
        used.append((col, slot))
        xgv[col, slot] = back_product(ccat[pl.ds(0, tok)], block)

    def product(slot):
        arrived(("xs", "cot"))
        arrived(("xs", slot))
        loaded("cot")
        loaded((0, slot))
        gbuf[slot] = lax.dot_general(
            acat[slot], ccat[...], (((0,), (0,)), ((), ())), preferred_element_type=F32
        )

    def reduce_send(direction, step, part):
        span = pl.ds(part * half, half)
        slot = HOPS - step if direction == 0 else HOPS + step
        value = gbuf[slot, :, span]
        if ("rs", direction, step - 1, part) in copies:
            arrived(("rs", direction, step - 1, part))
            value = value + rs_in[direction, step - 1, :, span].astype(F32)
        rs_out[direction, step, :, span] = value.astype(BF)
        copies["rs", direction, step, part].start()

    def finish(part):
        span = pl.ds(part * half, half)
        for name in ("first", "second", "w"):
            loaded(name)
        grad = gbuf[0, :, span]
        for direction in range(2):
            arrived(("rs", direction, HOPS - 1, part))
            grad = grad + rs_in[direction, HOPS - 1, :, span].astype(F32)
        new_a = beta_one * mom[0, :, span] + (1.0 - beta_one) * grad
        new_b = beta_two * mom[1, :, span] + (1.0 - beta_two) * grad * grad
        first_new[:, span] = new_a
        second_new[:, span] = new_b
        old = wg[0, 0, :, span].astype(F32)
        update = new_a / corr_one / (jnp.sqrt(new_b / corr_two) + adam_eps) + weight_decay * old
        stepped[part] = (old - learn_rate * update).astype(BF).reshape(stepped.shape[1:])

    def exchange_first(part):
        for copy in ex[0, part]:
            copy.start()
        inbox[part][rep] = stepped[part, rep]

    def exchange_second(part):
        loaded("partner")
        for copy in ex[0, part]:
            copy.wait_recv()
        for j in range(n_rep):
            outbox[part, j] = inbox[part][partner_s[j]]
        for copy in ex[1, part]:
            copy.start()
        final[part, rep] = outbox[part, rep]

    barrier = pltpu.get_barrier_semaphore()
    others = [(lax.rem(rep + k, n_rep), me) for k in range(1, n_rep)]
    for device in (up, down, side, *others):
        pl.semaphore_signal(barrier, inc=1, device_id=device, device_id_type=MESH)
    loads["cot"].start()
    loads["w"].start()
    for slot in (0, 7, 1, 4, 3, 5, 2, 6):
        loads[0, slot].start()
    pl.semaphore_wait(barrier, 3 + n_rep - 1)

    actions = {
        "use": use_block, "g": product, "rs": reduce_send, "fin": finish,
        "ex0": exchange_first, "ex1": exchange_second,
    }
    for position, token in enumerate(SCHEDULE):
        if position == LATE_LOADS:
            for slot in range(NZ):
                loads[1, slot].start()
            for name in ("first", "second", "partner"):
                loads[name].start()
        name = token[0]
        if name in actions:
            actions[name](*token[1:])
            continue
        if name == "ag":
            _, col, direction, hop = token
            if hop > 1:
                arrived(("ag", col, direction, hop - 1))
            elif col == 1:
                arrived(("wxB",))
        elif name == "wx":
            block_arrived(0, token[1])
        copies[token].start()

    for key, copy in copies.items():
        arrived(key)
        copy.wait_send()
    for part in range(2):
        for copy in ex[1, part]:
            copy.wait_recv()
        for phase in range(2):
            for copy in ex[phase, part]:
                copy.wait_send()
    for key in loads:
        loaded(key)


LATE_LOADS = 12
LEFT = tuple(
    (col, slot)
    for slot in (0, 7, 1, 6, 2, 5, 3, 4)
    for col in range(2)
    if ("use", col, slot) not in SCHEDULE
)


def write_out(
    kvacc, xgv, first_new, second_new, stepped, final, wg, aoth, ccat, mix_h,
    kv_h, xg_h, nw_h, nf_h, ns_h,
    kvb, xgl, nwv, mix_s, xg_sem, sem,
):
    tok = kvb.shape[0]
    rows, cols = nwv.shape
    half = cols // 2
    mix_load = pltpu.make_async_copy(mix_h, mix_s, sem.at[4])
    mix_load.start()
    copies = [
        pltpu.make_async_copy(first_new, nf_h, sem.at[0]),
        pltpu.make_async_copy(second_new, ns_h, sem.at[1]),
    ]
    for col in range(2):
        for slot in range(NZ):
            if (col, slot) not in LEFT:
                copies.append(
                    pltpu.make_async_copy(
                        xgv.at[col, slot], columns_of(xg_h, col, slot, rows), xg_sem.at[col, slot]
                    )
                )
    for copy in copies:
        copy.start()
    total = kvacc[...]
    for i, (col, slot) in enumerate(LEFT):
        block = wg[col, slot]
        total = total + jnp.dot(aoth[slot], block, preferred_element_type=F32)
        xgl[i] = back_product(ccat[pl.ds(0, tok)], block)
        copy = pltpu.make_async_copy(
            xgl.at[i], columns_of(xg_h, col, slot, rows), xg_sem.at[col, slot]
        )
        copy.start()
        copies.append(copy)
    kvb[...] = total.astype(BF)
    copies.append(pltpu.make_async_copy(kvb, kv_h, sem.at[2]))
    copies[-1].start()
    mix_load.wait()
    mixing = mix_s[lax.axis_index("rep")].astype(F32) / mix_denom
    for part in range(2):
        nwv[:, pl.ds(part * half, half)] = (
            ((1.0 - mixing) * stepped[part].astype(F32) + mixing * final[part].astype(F32))
            .astype(BF)
            .reshape(rows, half)
        )
    copies.append(pltpu.make_async_copy(nwv, nw_h, sem.at[3]))
    copies[-1].start()
    for copy in copies:
        copy.wait()


def per_device(
    activations, kv_weight, kv_cotangent, first_moment, second_moment, partner, mix_numerator
):
    act, weights, cot = activations[0], kv_weight[0], kv_cotangent[0]
    tok, width = act.shape
    rows, cols = weights.shape
    n_rep = partner.shape[0]
    chunks = (2, n_rep, rows // n_rep, cols // 2)
    dma = pltpu.SemaphoreType.DMA
    hbm = pl.BlockSpec(memory_space=pltpu.HBM)
    vmem = pl.BlockSpec(memory_space=pltpu.VMEM)

    def in_hbm(x):
        return pltpu.with_memory_space_constraint(x, pltpu.HBM)

    held = pl.pallas_call(
        kernel,
        out_shape=(
            pltpu.VMEM((tok, cols), F32),
            pltpu.VMEM((2, NZ, tok, rows), BF),
            pltpu.VMEM((rows, cols), F32),
            pltpu.VMEM((rows, cols), F32),
            pltpu.VMEM(chunks, BF),
            pltpu.VMEM(chunks, BF),
            pltpu.VMEM((2, NZ, rows, cols), BF),
            pltpu.VMEM((NZ, tok, rows), BF),
            pltpu.VMEM((2 * tok, cols), BF),
        ),
        in_specs=[hbm] * 6,
        out_specs=[vmem] * 9,
        scratch_shapes=[
            pltpu.VMEM((NZ, 2 * tok, rows), BF),
            pltpu.VMEM((2, rows, cols), F32),
            pltpu.VMEM((2, HOPS, rows, cols), BF),
            pltpu.VMEM((2, HOPS, rows, cols), BF),
            pltpu.VMEM((NZ, rows, cols), F32),
            pltpu.VMEM(chunks[1:], BF),
            pltpu.VMEM(chunks[1:], BF),
            pltpu.VMEM(chunks, BF),
            pltpu.SMEM((n_rep,), jnp.int32),
            dma((5,)),
            dma((2, NZ)),
            dma((NZ + 1,)),
            dma((NZ + 1,)),
            dma((NZ + 1,)),
            dma((NZ + 1,)),
            dma((2, 2, HOPS)),
            dma((2, 2, HOPS)),
            dma((2, HOPS, 2)),
            dma((2, HOPS, 2)),
            dma((2, 2, n_rep)),
            dma((2, 2, n_rep)),
        ],
        name="step",
        compiler_params=pltpu.CompilerParams(
            collective_id=0, has_side_effects=True, vmem_limit_bytes=32 << 20
        ),
    )(*(in_hbm(x) for x in (act, weights, cot, first_moment[0], second_moment[0], partner)))
    outs = pl.pallas_call(
        write_out,
        out_shape=(
            jax.ShapeDtypeStruct((tok, cols), BF),
            jax.ShapeDtypeStruct((tok, width), BF),
            jax.ShapeDtypeStruct((rows, cols), BF),
            jax.ShapeDtypeStruct((rows, cols), F32),
            jax.ShapeDtypeStruct((rows, cols), F32),
        ),
        in_specs=[vmem] * 9 + [hbm],
        out_specs=[hbm] * 5,
        scratch_shapes=[
            pltpu.VMEM((tok, cols), BF),
            pltpu.VMEM((len(LEFT), tok, rows), BF),
            pltpu.VMEM((rows, cols), BF),
            pltpu.SMEM((n_rep,), jnp.int32),
            dma((2, NZ)),
            dma((5,)),
        ],
        name="write_out",
        compiler_params=pltpu.CompilerParams(vmem_limit_bytes=8 << 20),
    )(*held, in_hbm(mix_numerator))
    return tuple(out[None] for out in outs)


def solution(mesh):
    split = P("rep", "fsdp", None)
    return jax.shard_map(
        per_device,
        mesh=mesh,
        in_specs=(split,) * 5 + (P(), P()),
        out_specs=(split,) * 5,
        check_vma=False,
    )
```

```python
import jax
import jax.numpy as jnp
from jax import lax
from jax.experimental import pallas as pl
from jax.experimental.pallas import tpu as pltpu
from jax.sharding import PartitionSpec as P

beta_one = 0.9
beta_two = 0.999
learn_rate = 0.02
weight_decay = 0.1
adam_eps = 1e-08
corr_one = 1.0 - beta_one**10
corr_two = 1.0 - beta_two**10
mix_denom = 64.0

MESH = pl.DeviceIdType.MESH
BF = jnp.bfloat16
F32 = jnp.float32
NZ = 8
HOPS = NZ // 2
ROWS_X = 96

SCHEDULE = (
    ("wxB",), ("ag", 0, 1, 1, 0), ("ag", 0, 0, 1, 0), ("ag", 0, 0, 1, 1), ("xs", 4),
    ("ag", 0, 1, 1, 1), ("ag", 0, 1, 2, 0), ("xs", 3), ("ag", 1, 0, 1, 0), ("ag", 1, 1, 1, 0),
    ("xs", "cot"), ("ag", 0, 1, 2, 1), ("ag", 1, 1, 1, 1), ("ag", 0, 0, 2, 0),
    ("ag", 1, 0, 2, 0), ("wxA",), ("ag", 0, 0, 2, 1), ("ag", 0, 1, 3, 0), ("xs", 5), ("xs", 2),
    ("ag", 0, 0, 3, 0), ("xs", 1), ("xs", 6), ("ag", 1, 1, 2, 1), ("g", 4), ("rs", 0, 0, 0),
    ("rs", 1, 0, 1), ("ag", 1, 0, 1, 1), ("xs", 0), ("g", 3), ("g", 5), ("rs", 0, 1, 0),
    ("xs", 7), ("rs", 1, 1, 0), ("rs", 0, 1, 1), ("g", 2), ("rs", 1, 1, 1), ("use", 0, 0),
    ("rs", 0, 2, 0), ("g", 1), ("ag", 0, 1, 3, 1), ("g", 6), ("rs", 1, 2, 1), ("rs", 1, 2, 0),
    ("rs", 0, 2, 1), ("use", 0, 2), ("g", 0), ("use", 0, 6), ("ag", 1, 0, 2, 1), ("wx", 7),
    ("use", 1, 0), ("wx", 6), ("use", 1, 7), ("rs", 0, 3, 1), ("wx", 3), ("wx", 2), ("g", 7),
    ("rs", 1, 3, 1), ("use", 1, 6), ("use", 0, 3), ("rs", 1, 3, 0), ("rs", 0, 3, 0),
    ("ag", 0, 0, 4, 0), ("ag", 1, 1, 2, 0), ("wx", 5), ("wx", 1), ("ag", 1, 1, 3, 1),
    ("ag", 0, 0, 3, 1), ("fin", 1), ("ag", 1, 0, 3, 0), ("ex0", 1), ("use", 0, 7), ("fin", 0),
    ("ag", 0, 1, 4, 1), ("ex0", 0), ("ag", 1, 0, 3, 1), ("use", 0, 1), ("wx", 4),
    ("ag", 1, 1, 4, 1), ("ex1", 1), ("ex1", 0), ("ag", 1, 0, 4, 0), ("use", 1, 1),
    ("ag", 1, 1, 3, 0), ("use", 1, 2), ("use", 0, 5), ("use", 0, 4), ("use", 1, 5),
    ("use", 1, 3),
)


def column_index(col, slot):
    me = lax.axis_index("fsdp")
    x = me % 2
    return lax.rem(me // 2 + slot, NZ) * 2 + (x if col == 0 else 1 - x)


def columns_of(ref, col, slot, rows):
    start = column_index(col, slot) * rows
    return ref.at[:, pl.ds(pl.multiple_of(start, rows), rows)]


def back_product(cot, block):
    return lax.dot_general(
        cot, block, (((1,), (1,)), ((), ())), preferred_element_type=F32
    ).astype(BF)


def kernel(
    act_h, w_h, cot_h, first_h, second_h, partner_h,
    kvacc, xgv, first_new, second_new, stepped, final, wg, aoth, ccat,
    acat, mom, rs_in, rs_out, gbuf, inbox_a, inbox_b, outbox, partner_s,
    load_sem, act_sem, x_send, x_recv, wx_send, wx_recv, ag_send, ag_recv,
    rs_send, rs_recv, ex_send, ex_recv,
):
    rep = lax.axis_index("rep")
    me = lax.axis_index("fsdp")
    inbox = (inbox_a, inbox_b)
    n_rep = inbox_a.shape[0]
    tok = cot_h.shape[0]
    rows, cols = w_h.shape
    half = cols // 2
    z, xl = me // 2, me % 2
    up = (rep, lax.rem(z + 1, NZ) * 2 + xl)
    down = (rep, lax.rem(z + NZ - 1, NZ) * 2 + xl)
    side = (rep, z * 2 + 1 - xl)
    ring = (up, down)

    def remote(src, dst, send, recv, target):
        return pltpu.make_async_remote_copy(
            src_ref=src, dst_ref=dst, send_sem=send, recv_sem=recv,
            device_id=target, device_id_type=MESH,
        )

    loads = {
        "cot": pltpu.make_async_copy(cot_h, ccat.at[pl.ds(0, tok)], load_sem.at[0]),
        "w": pltpu.make_async_copy(w_h, wg.at[0, 0], load_sem.at[1]),
        "first": pltpu.make_async_copy(first_h, mom.at[0], load_sem.at[2]),
        "second": pltpu.make_async_copy(second_h, mom.at[1], load_sem.at[3]),
        "partner": pltpu.make_async_copy(partner_h, partner_s, load_sem.at[4]),
    }
    for slot in range(NZ):
        loads[0, slot] = pltpu.make_async_copy(
            columns_of(act_h, 0, slot, rows), acat.at[slot, pl.ds(0, tok)], act_sem.at[0, slot]
        )
        loads[1, slot] = pltpu.make_async_copy(
            columns_of(act_h, 1, slot, rows), aoth.at[slot], act_sem.at[1, slot]
        )
    waited = set()

    def loaded(key):
        if key not in waited:
            waited.add(key)
            loads[key].wait()

    copies = {
        ("xs", "cot"): remote(
            cot_h, ccat.at[pl.ds(tok, tok)], x_send.at[NZ], x_recv.at[NZ], side
        ),
        ("wxA",): remote(
            w_h.at[pl.ds(0, ROWS_X)], wg.at[1, 0, pl.ds(0, ROWS_X)],
            wx_send.at[0], wx_recv.at[0], side,
        ),
        ("wxB",): remote(
            w_h.at[pl.ds(ROWS_X, rows - ROWS_X)], wg.at[1, 0, pl.ds(ROWS_X, rows - ROWS_X)],
            wx_send.at[NZ], wx_recv.at[NZ], side,
        ),
    }
    for slot in range(NZ):
        copies["xs", slot] = remote(
            columns_of(act_h, 1, slot, rows), acat.at[slot, pl.ds(tok, tok)],
            x_send.at[slot], x_recv.at[slot], side,
        )
        if slot > 0:
            copies["wx", slot] = remote(
                wg.at[0, slot, pl.ds(0, ROWS_X)], wg.at[1, slot, pl.ds(0, ROWS_X)],
                wx_send.at[slot], wx_recv.at[slot], side,
            )

    def gather(col, direction, hop, part):
        low, high = (0, rows) if col == 0 else (ROWS_X, rows)
        length = (high - low) // 2
        span = pl.ds(low + part * length, length)
        if direction == 0:
            src, dst = (NZ - hop + 1) % NZ, NZ - hop
        else:
            src, dst = hop - 1, hop
        source = w_h.at[span] if (col == 0 and hop == 1) else wg.at[col, src, span]
        sems = (col, direction, hop - 1, part)
        return remote(
            source, wg.at[col, dst, span], ag_send.at[sems], ag_recv.at[sems], ring[direction]
        )

    def reduce_copy(direction, step, part):
        span = (direction, step, slice(None), pl.ds(part * half, half))
        return remote(
            rs_out.at[span], rs_in.at[span],
            rs_send.at[direction, step, part], rs_recv.at[direction, step, part],
            ring[direction],
        )

    for direction in range(2):
        for hop in range(1, HOPS + 1):
            for col in range(2):
                for part in range(2):
                    if hop < HOPS or part == direction:
                        token = ("ag", col, direction, hop, part)
                        copies[token] = gather(*token[1:])
        for step in range(HOPS):
            for part in range(2):
                if step > 0 or part == direction:
                    copies["rs", direction, step, part] = reduce_copy(direction, step, part)

    def exchange(phase, part):
        out = []
        for k in range(1, n_rep):
            peer = lax.rem(rep + k, n_rep)
            src = (stepped, outbox)[phase].at[part, peer]
            dst = final.at[part, rep] if phase else inbox[part].at[rep]
            out.append(
                remote(
                    src, dst,
                    ex_send.at[phase, part, k], ex_recv.at[phase, part, k], (peer, me),
                )
            )
        return out

    ex = {(phase, part): exchange(phase, part) for phase in range(2) for part in range(2)}

    def arrived(key):
        if key not in waited:
            waited.add(key)
            copies[key].wait_recv()

    def block_arrived(col, slot, parts=(0, 1)):
        for part in parts:
            if slot == 0:
                if col == 1:
                    arrived(("wxB",))
            elif slot == HOPS:
                arrived(("ag", col, part, HOPS, part))
            elif slot > HOPS:
                arrived(("ag", col, 0, NZ - slot, part))
            else:
                arrived(("ag", col, 1, slot, part))

    used = []

    def use_block(col, slot):
        block_arrived(col, slot)
        if col == 1:
            arrived(("wx", slot) if slot else ("wxA",))
        elif slot == 0:
            loaded("w")
        loaded("cot")
        loaded((col, slot))
        block = wg[col, slot]
        tokens = acat[slot, pl.ds(0, tok)] if col == 0 else aoth[slot]
        term = jnp.dot(tokens, block, preferred_element_type=F32)
        if used:
            kvacc[...] += term
        else:
            kvacc[...] = term
        used.append((col, slot))
        xgv[col, slot] = back_product(ccat[pl.ds(0, tok)], block)

    def product(slot):
        arrived(("xs", "cot"))
        arrived(("xs", slot))
        loaded("cot")
        loaded((0, slot))
        gbuf[slot] = lax.dot_general(
            acat[slot], ccat[...], (((0,), (0,)), ((), ())), preferred_element_type=F32
        )

    def reduce_send(direction, step, part):
        span = pl.ds(part * half, half)
        slot = HOPS - step if direction == 0 else HOPS + step
        value = gbuf[slot, :, span]
        if ("rs", direction, step - 1, part) in copies:
            arrived(("rs", direction, step - 1, part))
            value = value + rs_in[direction, step - 1, :, span].astype(F32)
        rs_out[direction, step, :, span] = value.astype(BF)
        copies["rs", direction, step, part].start()

    def finish(part):
        span = pl.ds(part * half, half)
        for name in ("first", "second", "w"):
            loaded(name)
        grad = gbuf[0, :, span]
        for direction in range(2):
            arrived(("rs", direction, HOPS - 1, part))
            grad = grad + rs_in[direction, HOPS - 1, :, span].astype(F32)
        new_a = beta_one * mom[0, :, span] + (1.0 - beta_one) * grad
        new_b = beta_two * mom[1, :, span] + (1.0 - beta_two) * grad * grad
        first_new[:, span] = new_a
        second_new[:, span] = new_b
        old = wg[0, 0, :, span].astype(F32)
        update = new_a / corr_one / (jnp.sqrt(new_b / corr_two) + adam_eps) + weight_decay * old
        stepped[part] = (old - learn_rate * update).astype(BF).reshape(stepped.shape[1:])

    def exchange_first(part):
        for copy in ex[0, part]:
            copy.start()
        inbox[part][rep] = stepped[part, rep]

    def exchange_second(part):
        loaded("partner")
        for copy in ex[0, part]:
            copy.wait_recv()
        for j in range(n_rep):
            outbox[part, j] = inbox[part][partner_s[j]]
        for copy in ex[1, part]:
            copy.start()
        final[part, rep] = outbox[part, rep]

    barrier = pltpu.get_barrier_semaphore()
    others = [(lax.rem(rep + k, n_rep), me) for k in range(1, n_rep)]
    for device in (up, down, side, *others):
        pl.semaphore_signal(barrier, inc=1, device_id=device, device_id_type=MESH)
    loads["cot"].start()
    loads["w"].start()
    for slot in (0, 7, 1, 4, 3, 5, 2, 6):
        loads[0, slot].start()
    pl.semaphore_wait(barrier, 3 + n_rep - 1)

    actions = {
        "use": use_block, "g": product, "rs": reduce_send, "fin": finish,
        "ex0": exchange_first, "ex1": exchange_second,
    }
    for position, token in enumerate(SCHEDULE):
        if position == LATE_LOADS:
            for slot in range(NZ):
                loads[1, slot].start()
            for name in ("first", "second", "partner"):
                loads[name].start()
        name = token[0]
        if name in actions:
            actions[name](*token[1:])
            continue
        if name == "ag":
            _, col, direction, hop, part = token
            if hop > 1:
                arrived(("ag", col, direction, hop - 1, part))
            elif col == 1:
                arrived(("wxB",))
        elif name == "wx":
            block_arrived(0, token[1], (0,))
        copies[token].start()

    for key, copy in copies.items():
        arrived(key)
        copy.wait_send()
    for part in range(2):
        for copy in ex[1, part]:
            copy.wait_recv()
        for phase in range(2):
            for copy in ex[phase, part]:
                copy.wait_send()
    for key in loads:
        loaded(key)


LATE_LOADS = 16
LEFT = tuple(
    (col, slot)
    for slot in (0, 7, 1, 6, 2, 5, 3, 4)
    for col in range(2)
    if ("use", col, slot) not in SCHEDULE
)


def write_out(
    kvacc, xgv, first_new, second_new, stepped, final, wg, aoth, ccat, mix_h,
    kv_h, xg_h, nw_h, nf_h, ns_h,
    kvb, xgl, nwv, mix_s, xg_sem, sem,
):
    tok = kvb.shape[0]
    rows, cols = nwv.shape
    half = cols // 2
    mix_load = pltpu.make_async_copy(mix_h, mix_s, sem.at[4])
    mix_load.start()
    copies = [
        pltpu.make_async_copy(first_new, nf_h, sem.at[0]),
        pltpu.make_async_copy(second_new, ns_h, sem.at[1]),
    ]
    for col in range(2):
        for slot in range(NZ):
            if (col, slot) not in LEFT:
                copies.append(
                    pltpu.make_async_copy(
                        xgv.at[col, slot], columns_of(xg_h, col, slot, rows), xg_sem.at[col, slot]
                    )
                )
    for copy in copies:
        copy.start()
    total = kvacc[...]
    for i, (col, slot) in enumerate(LEFT):
        block = wg[col, slot]
        total = total + jnp.dot(aoth[slot], block, preferred_element_type=F32)
        xgl[i] = back_product(ccat[pl.ds(0, tok)], block)
        copy = pltpu.make_async_copy(
            xgl.at[i], columns_of(xg_h, col, slot, rows), xg_sem.at[col, slot]
        )
        copy.start()
        copies.append(copy)
    kvb[...] = total.astype(BF)
    copies.append(pltpu.make_async_copy(kvb, kv_h, sem.at[2]))
    copies[-1].start()
    mix_load.wait()
    mixing = mix_s[lax.axis_index("rep")].astype(F32) / mix_denom
    for part in range(2):
        nwv[:, pl.ds(part * half, half)] = (
            ((1.0 - mixing) * stepped[part].astype(F32) + mixing * final[part].astype(F32))
            .astype(BF)
            .reshape(rows, half)
        )
    copies.append(pltpu.make_async_copy(nwv, nw_h, sem.at[3]))
    copies[-1].start()
    for copy in copies:
        copy.wait()


def per_device(
    activations, kv_weight, kv_cotangent, first_moment, second_moment, partner, mix_numerator
):
    act, weights, cot = activations[0], kv_weight[0], kv_cotangent[0]
    tok, width = act.shape
    rows, cols = weights.shape
    n_rep = partner.shape[0]
    chunks = (2, n_rep, rows // n_rep, cols // 2)
    dma = pltpu.SemaphoreType.DMA
    hbm = pl.BlockSpec(memory_space=pltpu.HBM)
    vmem = pl.BlockSpec(memory_space=pltpu.VMEM)

    def in_hbm(x):
        return pltpu.with_memory_space_constraint(x, pltpu.HBM)

    held = pl.pallas_call(
        kernel,
        out_shape=(
            pltpu.VMEM((tok, cols), F32),
            pltpu.VMEM((2, NZ, tok, rows), BF),
            pltpu.VMEM((rows, cols), F32),
            pltpu.VMEM((rows, cols), F32),
            pltpu.VMEM(chunks, BF),
            pltpu.VMEM(chunks, BF),
            pltpu.VMEM((2, NZ, rows, cols), BF),
            pltpu.VMEM((NZ, tok, rows), BF),
            pltpu.VMEM((2 * tok, cols), BF),
        ),
        in_specs=[hbm] * 6,
        out_specs=[vmem] * 9,
        scratch_shapes=[
            pltpu.VMEM((NZ, 2 * tok, rows), BF),
            pltpu.VMEM((2, rows, cols), F32),
            pltpu.VMEM((2, HOPS, rows, cols), BF),
            pltpu.VMEM((2, HOPS, rows, cols), BF),
            pltpu.VMEM((NZ, rows, cols), F32),
            pltpu.VMEM(chunks[1:], BF),
            pltpu.VMEM(chunks[1:], BF),
            pltpu.VMEM(chunks, BF),
            pltpu.SMEM((n_rep,), jnp.int32),
            dma((5,)),
            dma((2, NZ)),
            dma((NZ + 1,)),
            dma((NZ + 1,)),
            dma((NZ + 1,)),
            dma((NZ + 1,)),
            dma((2, 2, HOPS, 2)),
            dma((2, 2, HOPS, 2)),
            dma((2, HOPS, 2)),
            dma((2, HOPS, 2)),
            dma((2, 2, n_rep)),
            dma((2, 2, n_rep)),
        ],
        name="step",
        compiler_params=pltpu.CompilerParams(
            collective_id=0, has_side_effects=True, vmem_limit_bytes=32 << 20
        ),
    )(*(in_hbm(x) for x in (act, weights, cot, first_moment[0], second_moment[0], partner)))
    outs = pl.pallas_call(
        write_out,
        out_shape=(
            jax.ShapeDtypeStruct((tok, cols), BF),
            jax.ShapeDtypeStruct((tok, width), BF),
            jax.ShapeDtypeStruct((rows, cols), BF),
            jax.ShapeDtypeStruct((rows, cols), F32),
            jax.ShapeDtypeStruct((rows, cols), F32),
        ),
        in_specs=[vmem] * 9 + [hbm],
        out_specs=[hbm] * 5,
        scratch_shapes=[
            pltpu.VMEM((tok, cols), BF),
            pltpu.VMEM((len(LEFT), tok, rows), BF),
            pltpu.VMEM((rows, cols), BF),
            pltpu.SMEM((n_rep,), jnp.int32),
            dma((2, NZ)),
            dma((5,)),
        ],
        name="write_out",
        compiler_params=pltpu.CompilerParams(vmem_limit_bytes=8 << 20),
    )(*held, in_hbm(mix_numerator))
    return tuple(out[None] for out in outs)


def solution(mesh):
    split = P("rep", "fsdp", None)
    return jax.shard_map(
        per_device,
        mesh=mesh,
        in_specs=(split,) * 5 + (P(), P()),
        out_specs=(split,) * 5,
        check_vma=False,
    )
```

```python
import jax
import jax.numpy as jnp
from jax import lax
from jax.experimental import pallas as pl
from jax.experimental.pallas import tpu as pltpu
from jax.sharding import PartitionSpec as P

beta_one = 0.9
beta_two = 0.999
learn_rate = 0.02
weight_decay = 0.1
adam_eps = 1e-08
corr_one = 1.0 - beta_one**10
corr_two = 1.0 - beta_two**10
mix_denom = 64.0

MESH = pl.DeviceIdType.MESH
BF = jnp.bfloat16
F32 = jnp.float32
NZ = 8
HOPS = NZ // 2
ROWS_X = 96

SCHEDULE = (
    ("wxB",), ("ag", 0, 0, 1, 0), ("ag", 0, 1, 1, 0), ("xs", "cot"), ("xs", 4), ("xs", 3),
    ("ag", 0, 1, 1, 1), ("xs", 5), ("ag", 0, 0, 1, 1), ("xs", 2), ("ag", 0, 0, 2, 0), ("xs", 1),
    ("ag", 0, 1, 2, 0), ("wxA",), ("ag", 1, 1, 1, 1), ("ag", 1, 0, 1, 0), ("ag", 0, 1, 2, 1),
    ("ag", 0, 0, 2, 1), ("ag", 1, 0, 1, 1), ("ag", 0, 1, 3, 0), ("xs", 6), ("xs", 7),
    ("ag", 1, 1, 1, 0), ("ag", 0, 0, 3, 0), ("g", 4), ("rs", 0, 0, 0), ("rs", 1, 0, 1), ("g", 3),
    ("rs", 0, 1, 1), ("ag", 1, 1, 2, 1), ("g", 5), ("rs", 1, 1, 0), ("ag", 1, 0, 2, 0),
    ("rs", 1, 1, 1), ("wx", 7), ("g", 2), ("ag", 0, 1, 3, 1), ("rs", 0, 1, 0), ("g", 1),
    ("rs", 0, 2, 1), ("g", 6), ("rs", 1, 2, 1), ("rs", 0, 2, 0), ("xs", 0), ("g", 7),
    ("ag", 0, 0, 3, 1), ("use", 0, 0), ("wx", 1), ("wx", 6), ("wx", 5), ("rs", 1, 2, 0),
    ("use", 0, 2), ("use", 0, 6), ("rs", 0, 3, 1), ("rs", 1, 3, 1), ("rs", 0, 3, 0), ("g", 0),
    ("rs", 1, 3, 0), ("ag", 1, 1, 2, 0), ("ag", 1, 1, 3, 1), ("ag", 0, 0, 4, 0), ("wx", 2),
    ("ag", 1, 0, 2, 1), ("wx", 3), ("use", 0, 3), ("use", 0, 1), ("use", 1, 7), ("use", 0, 7),
    ("ag", 1, 0, 3, 0), ("use", 1, 0), ("fin", 1), ("ex0", 1), ("use", 0, 5), ("ag", 0, 1, 4, 1),
    ("fin", 0), ("ex0", 0), ("ag", 1, 1, 3, 0), ("wx", 4), ("use", 1, 1), ("ex1", 1),
    ("ag", 1, 0, 3, 1), ("ex1", 0), ("ag", 1, 0, 4, 0), ("ag", 1, 1, 4, 1), ("use", 1, 6),
    ("use", 1, 2), ("use", 0, 4), ("use", 1, 5), ("use", 1, 3),
)


def column_index(col, slot):
    me = lax.axis_index("fsdp")
    x = me % 2
    return lax.rem(me // 2 + slot, NZ) * 2 + (x if col == 0 else 1 - x)


def columns_of(ref, col, slot, rows):
    start = column_index(col, slot) * rows
    return ref.at[:, pl.ds(pl.multiple_of(start, rows), rows)]


def back_product(cot, block):
    return lax.dot_general(
        cot, block, (((1,), (1,)), ((), ())), preferred_element_type=F32
    ).astype(BF)


def kernel(
    act_h, w_h, cot_h, first_h, second_h, partner_h,
    kvacc, xgv, first_new, second_new, stepped, final, wg, aoth, ccat,
    acat, mom, rs_in, rs_out, gbuf, inbox_a, inbox_b, outbox, partner_s,
    load_sem, act_sem, x_send, x_recv, wx_send, wx_recv, ag_send, ag_recv,
    rs_send, rs_recv, ex_send, ex_recv,
):
    rep = lax.axis_index("rep")
    me = lax.axis_index("fsdp")
    inbox = (inbox_a, inbox_b)
    n_rep = inbox_a.shape[0]
    tok = cot_h.shape[0]
    rows, cols = w_h.shape
    half = cols // 2
    z, xl = me // 2, me % 2
    up = (rep, lax.rem(z + 1, NZ) * 2 + xl)
    down = (rep, lax.rem(z + NZ - 1, NZ) * 2 + xl)
    side = (rep, z * 2 + 1 - xl)
    ring = (up, down)

    def remote(src, dst, send, recv, target):
        return pltpu.make_async_remote_copy(
            src_ref=src, dst_ref=dst, send_sem=send, recv_sem=recv,
            device_id=target, device_id_type=MESH,
        )

    loads = {
        "cot": pltpu.make_async_copy(cot_h, ccat.at[pl.ds(0, tok)], load_sem.at[0]),
        "w": pltpu.make_async_copy(w_h, wg.at[0, 0], load_sem.at[1]),
        "first": pltpu.make_async_copy(first_h, mom.at[0], load_sem.at[2]),
        "second": pltpu.make_async_copy(second_h, mom.at[1], load_sem.at[3]),
        "partner": pltpu.make_async_copy(partner_h, partner_s, load_sem.at[4]),
    }
    for slot in range(NZ):
        loads[0, slot] = pltpu.make_async_copy(
            columns_of(act_h, 0, slot, rows), acat.at[slot, pl.ds(0, tok)], act_sem.at[0, slot]
        )
        loads[1, slot] = pltpu.make_async_copy(
            columns_of(act_h, 1, slot, rows), aoth.at[slot], act_sem.at[1, slot]
        )
    waited = set()

    def loaded(key):
        if key not in waited:
            waited.add(key)
            loads[key].wait()

    copies = {
        ("xs", "cot"): remote(
            cot_h, ccat.at[pl.ds(tok, tok)], x_send.at[NZ], x_recv.at[NZ], side
        ),
        ("wxA",): remote(
            w_h.at[pl.ds(0, ROWS_X)], wg.at[1, 0, pl.ds(0, ROWS_X)],
            wx_send.at[0], wx_recv.at[0], side,
        ),
        ("wxB",): remote(
            w_h.at[pl.ds(ROWS_X, rows - ROWS_X)], wg.at[1, 0, pl.ds(ROWS_X, rows - ROWS_X)],
            wx_send.at[NZ], wx_recv.at[NZ], side,
        ),
    }
    for slot in range(NZ):
        copies["xs", slot] = remote(
            columns_of(act_h, 1, slot, rows), acat.at[slot, pl.ds(tok, tok)],
            x_send.at[slot], x_recv.at[slot], side,
        )
        if slot > 0:
            copies["wx", slot] = remote(
                wg.at[0, slot, pl.ds(0, ROWS_X)], wg.at[1, slot, pl.ds(0, ROWS_X)],
                wx_send.at[slot], wx_recv.at[slot], side,
            )

    def gather(col, direction, hop, part):
        low, high = (0, rows) if col == 0 else (ROWS_X, rows)
        length = (high - low) // 2
        span = pl.ds(low + part * length, length)
        if direction == 0:
            src, dst = (NZ - hop + 1) % NZ, NZ - hop
        else:
            src, dst = hop - 1, hop
        source = w_h.at[span] if (col == 0 and hop == 1) else wg.at[col, src, span]
        sems = (col, direction, hop - 1, part)
        return remote(
            source, wg.at[col, dst, span], ag_send.at[sems], ag_recv.at[sems], ring[direction]
        )

    def reduce_copy(direction, step, part):
        span = (direction, step, slice(None), pl.ds(part * half, half))
        return remote(
            rs_out.at[span], rs_in.at[span],
            rs_send.at[direction, step, part], rs_recv.at[direction, step, part],
            ring[direction],
        )

    for direction in range(2):
        for hop in range(1, HOPS + 1):
            for col in range(2):
                for part in range(2):
                    if hop < HOPS or part == direction:
                        token = ("ag", col, direction, hop, part)
                        copies[token] = gather(*token[1:])
        for step in range(HOPS):
            for part in range(2):
                if step > 0 or part == direction:
                    copies["rs", direction, step, part] = reduce_copy(direction, step, part)

    def exchange(phase, part):
        out = []
        for k in range(1, n_rep):
            peer = lax.rem(rep + k, n_rep)
            src = (stepped, outbox)[phase].at[part, peer]
            dst = final.at[part, rep] if phase else inbox[part].at[rep]
            out.append(
                remote(
                    src, dst,
                    ex_send.at[phase, part, k], ex_recv.at[phase, part, k], (peer, me),
                )
            )
        return out

    ex = {(phase, part): exchange(phase, part) for phase in range(2) for part in range(2)}

    def arrived(key):
        if key not in waited:
            waited.add(key)
            copies[key].wait_recv()

    def block_arrived(col, slot, parts=(0, 1)):
        for part in parts:
            if slot == 0:
                if col == 1:
                    arrived(("wxB",))
            elif slot == HOPS:
                arrived(("ag", col, part, HOPS, part))
            elif slot > HOPS:
                arrived(("ag", col, 0, NZ - slot, part))
            else:
                arrived(("ag", col, 1, slot, part))

    used = []

    def use_block(col, slot):
        block_arrived(col, slot)
        if col == 1:
            arrived(("wx", slot) if slot else ("wxA",))
        elif slot == 0:
            loaded("w")
        loaded("cot")
        loaded((col, slot))
        block = wg[col, slot]
        tokens = acat[slot, pl.ds(0, tok)] if col == 0 else aoth[slot]
        term = jnp.dot(tokens, block, preferred_element_type=F32)
        if used:
            kvacc[...] += term
        else:
            kvacc[...] = term
        used.append((col, slot))
        xgv[col, slot] = back_product(ccat[pl.ds(0, tok)], block)

    def product(slot):
        arrived(("xs", "cot"))
        arrived(("xs", slot))
        loaded("cot")
        loaded((0, slot))
        gbuf[slot] = lax.dot_general(
            acat[slot], ccat[...], (((0,), (0,)), ((), ())), preferred_element_type=F32
        )

    def reduce_send(direction, step, part):
        span = pl.ds(part * half, half)
        slot = HOPS - step if direction == 0 else HOPS + step
        value = gbuf[slot, :, span]
        if ("rs", direction, step - 1, part) in copies:
            arrived(("rs", direction, step - 1, part))
            value = value + rs_in[direction, step - 1, :, span].astype(F32)
        rs_out[direction, step, :, span] = value.astype(BF)
        copies["rs", direction, step, part].start()

    def finish(part):
        span = pl.ds(part * half, half)
        for name in ("first", "second", "w"):
            loaded(name)
        grad = gbuf[0, :, span]
        for direction in range(2):
            arrived(("rs", direction, HOPS - 1, part))
            grad = grad + rs_in[direction, HOPS - 1, :, span].astype(F32)
        new_a = beta_one * mom[0, :, span] + (1.0 - beta_one) * grad
        new_b = beta_two * mom[1, :, span] + (1.0 - beta_two) * grad * grad
        first_new[:, span] = new_a
        second_new[:, span] = new_b
        old = wg[0, 0, :, span].astype(F32)
        update = new_a / corr_one / (jnp.sqrt(new_b / corr_two) + adam_eps) + weight_decay * old
        stepped[part] = (old - learn_rate * update).astype(BF).reshape(stepped.shape[1:])

    def exchange_first(part):
        for copy in ex[0, part]:
            copy.start()
        inbox[part][rep] = stepped[part, rep]

    def exchange_second(part):
        loaded("partner")
        for copy in ex[0, part]:
            copy.wait_recv()
        for j in range(n_rep):
            outbox[part, j] = inbox[part][partner_s[j]]
        for copy in ex[1, part]:
            copy.start()
        final[part, rep] = outbox[part, rep]

    barrier = pltpu.get_barrier_semaphore()
    others = [(lax.rem(rep + k, n_rep), me) for k in range(1, n_rep)]
    for device in (up, down, side, *others):
        pl.semaphore_signal(barrier, inc=1, device_id=device, device_id_type=MESH)
    loads["cot"].start()
    loads["w"].start()
    for slot in (0, 7, 1, 4, 3, 5, 2, 6):
        loads[0, slot].start()
    pl.semaphore_wait(barrier, 3 + n_rep - 1)

    actions = {
        "use": use_block, "g": product, "rs": reduce_send, "fin": finish,
        "ex0": exchange_first, "ex1": exchange_second,
    }
    for position, token in enumerate(SCHEDULE):
        if position == LATE_LOADS:
            for slot in range(NZ):
                loads[1, slot].start()
            for name in ("first", "second", "partner"):
                loads[name].start()
        name = token[0]
        if name in actions:
            actions[name](*token[1:])
            continue
        if name == "ag":
            _, col, direction, hop, part = token
            if hop > 1:
                arrived(("ag", col, direction, hop - 1, part))
            elif col == 1:
                arrived(("wxB",))
        elif name == "wx":
            block_arrived(0, token[1], (0,))
        copies[token].start()

    for key, copy in copies.items():
        arrived(key)
        copy.wait_send()
    for part in range(2):
        for copy in ex[1, part]:
            copy.wait_recv()
        for phase in range(2):
            for copy in ex[phase, part]:
                copy.wait_send()
    for key in loads:
        loaded(key)


LATE_LOADS = 16
LEFT = tuple(
    (col, slot)
    for slot in (0, 7, 1, 6, 2, 5, 3, 4)
    for col in range(2)
    if ("use", col, slot) not in SCHEDULE
)


def write_out(
    kvacc, xgv, first_new, second_new, stepped, final, wg, aoth, ccat, mix_h,
    kv_h, xg_h, nw_h, nf_h, ns_h,
    kvb, xgl, nwv, mix_s, xg_sem, sem,
):
    tok = kvb.shape[0]
    rows, cols = nwv.shape
    half = cols // 2
    mix_load = pltpu.make_async_copy(mix_h, mix_s, sem.at[4])
    mix_load.start()
    copies = [
        pltpu.make_async_copy(first_new, nf_h, sem.at[0]),
        pltpu.make_async_copy(second_new, ns_h, sem.at[1]),
    ]
    for col in range(2):
        for slot in range(NZ):
            if (col, slot) not in LEFT:
                copies.append(
                    pltpu.make_async_copy(
                        xgv.at[col, slot], columns_of(xg_h, col, slot, rows), xg_sem.at[col, slot]
                    )
                )
    for copy in copies:
        copy.start()
    total = kvacc[...]
    for i, (col, slot) in enumerate(LEFT):
        block = wg[col, slot]
        total = total + jnp.dot(aoth[slot], block, preferred_element_type=F32)
        xgl[i] = back_product(ccat[pl.ds(0, tok)], block)
        copy = pltpu.make_async_copy(
            xgl.at[i], columns_of(xg_h, col, slot, rows), xg_sem.at[col, slot]
        )
        copy.start()
        copies.append(copy)
    kvb[...] = total.astype(BF)
    copies.append(pltpu.make_async_copy(kvb, kv_h, sem.at[2]))
    copies[-1].start()
    mix_load.wait()
    mixing = mix_s[lax.axis_index("rep")].astype(F32) / mix_denom
    for part in range(2):
        nwv[:, pl.ds(part * half, half)] = (
            ((1.0 - mixing) * stepped[part].astype(F32) + mixing * final[part].astype(F32))
            .astype(BF)
            .reshape(rows, half)
        )
    copies.append(pltpu.make_async_copy(nwv, nw_h, sem.at[3]))
    copies[-1].start()
    for copy in copies:
        copy.wait()


def per_device(
    activations, kv_weight, kv_cotangent, first_moment, second_moment, partner, mix_numerator
):
    act, weights, cot = activations[0], kv_weight[0], kv_cotangent[0]
    tok, width = act.shape
    rows, cols = weights.shape
    n_rep = partner.shape[0]
    chunks = (2, n_rep, rows // n_rep, cols // 2)
    dma = pltpu.SemaphoreType.DMA
    hbm = pl.BlockSpec(memory_space=pltpu.HBM)
    vmem = pl.BlockSpec(memory_space=pltpu.VMEM)

    def in_hbm(x):
        return pltpu.with_memory_space_constraint(x, pltpu.HBM)

    held = pl.pallas_call(
        kernel,
        out_shape=(
            pltpu.VMEM((tok, cols), F32),
            pltpu.VMEM((2, NZ, tok, rows), BF),
            pltpu.VMEM((rows, cols), F32),
            pltpu.VMEM((rows, cols), F32),
            pltpu.VMEM(chunks, BF),
            pltpu.VMEM(chunks, BF),
            pltpu.VMEM((2, NZ, rows, cols), BF),
            pltpu.VMEM((NZ, tok, rows), BF),
            pltpu.VMEM((2 * tok, cols), BF),
        ),
        in_specs=[hbm] * 6,
        out_specs=[vmem] * 9,
        scratch_shapes=[
            pltpu.VMEM((NZ, 2 * tok, rows), BF),
            pltpu.VMEM((2, rows, cols), F32),
            pltpu.VMEM((2, HOPS, rows, cols), BF),
            pltpu.VMEM((2, HOPS, rows, cols), BF),
            pltpu.VMEM((NZ, rows, cols), F32),
            pltpu.VMEM(chunks[1:], BF),
            pltpu.VMEM(chunks[1:], BF),
            pltpu.VMEM(chunks, BF),
            pltpu.SMEM((n_rep,), jnp.int32),
            dma((5,)),
            dma((2, NZ)),
            dma((NZ + 1,)),
            dma((NZ + 1,)),
            dma((NZ + 1,)),
            dma((NZ + 1,)),
            dma((2, 2, HOPS, 2)),
            dma((2, 2, HOPS, 2)),
            dma((2, HOPS, 2)),
            dma((2, HOPS, 2)),
            dma((2, 2, n_rep)),
            dma((2, 2, n_rep)),
        ],
        name="step",
        compiler_params=pltpu.CompilerParams(
            collective_id=0, has_side_effects=True, vmem_limit_bytes=32 << 20
        ),
    )(*(in_hbm(x) for x in (act, weights, cot, first_moment[0], second_moment[0], partner)))
    outs = pl.pallas_call(
        write_out,
        out_shape=(
            jax.ShapeDtypeStruct((tok, cols), BF),
            jax.ShapeDtypeStruct((tok, width), BF),
            jax.ShapeDtypeStruct((rows, cols), BF),
            jax.ShapeDtypeStruct((rows, cols), F32),
            jax.ShapeDtypeStruct((rows, cols), F32),
        ),
        in_specs=[vmem] * 9 + [hbm],
        out_specs=[hbm] * 5,
        scratch_shapes=[
            pltpu.VMEM((tok, cols), BF),
            pltpu.VMEM((len(LEFT), tok, rows), BF),
            pltpu.VMEM((rows, cols), BF),
            pltpu.SMEM((n_rep,), jnp.int32),
            dma((2, NZ)),
            dma((5,)),
        ],
        name="write_out",
        compiler_params=pltpu.CompilerParams(vmem_limit_bytes=8 << 20),
    )(*held, in_hbm(mix_numerator))
    return tuple(out[None] for out in outs)


def solution(mesh):
    split = P("rep", "fsdp", None)
    return jax.shard_map(
        per_device,
        mesh=mesh,
        in_specs=(split,) * 5 + (P(), P()),
        out_specs=(split,) * 5,
        check_vma=False,
    )
```

```python
import jax
import jax.numpy as jnp
from jax import lax
from jax.experimental import pallas as pl
from jax.experimental.pallas import tpu as pltpu
from jax.sharding import PartitionSpec as P

beta_one = 0.9
beta_two = 0.999
learn_rate = 0.02
weight_decay = 0.1
adam_eps = 1e-08
corr_one = 1.0 - beta_one**10
corr_two = 1.0 - beta_two**10
mix_denom = 64.0

MESH = pl.DeviceIdType.MESH
BF = jnp.bfloat16
F32 = jnp.float32
NZ = 8
HOPS = NZ // 2

SCHEDULE = (
    ("xs", "cot"), ("xs", 4), ("xs", 3), ("ag", 0, 1, 1, 0), ("ag", 0, 0, 1, 1),
    ("ag", 0, 0, 1, 0), ("ag", 0, 1, 1, 1), ("xs", 5), ("ag", 0, 0, 2, 1), ("xs", 2), ("xs", 1),
    ("xs", 6), ("xs", 0), ("ag", 0, 1, 2, 0), ("ag", 0, 1, 2, 1), ("ag", 0, 0, 2, 0),
    ("ag", 0, 0, 3, 1), ("g", 4), ("rs", 1, 0, 1), ("ag", 0, 1, 3, 1), ("rs", 0, 0, 0), ("g", 5),
    ("rs", 1, 1, 1), ("xs", 7), ("wxB",), ("g", 3), ("rs", 0, 1, 1), ("use", 0, 7),
    ("rs", 1, 1, 0), ("rs", 0, 1, 0), ("use", 0, 0), ("g", 2), ("g", 1), ("g", 6),
    ("rs", 0, 2, 1), ("rs", 1, 2, 1), ("px", 6), ("px", 5), ("rs", 1, 2, 0), ("rs", 0, 2, 0),
    ("g", 7), ("g", 0), ("rs", 0, 3, 1), ("px", 2), ("rs", 1, 3, 1), ("use", 0, 6),
    ("rs", 1, 3, 0), ("px", 0), ("rs", 0, 3, 0), ("ag", 1, 0, 1, 1), ("ag", 1, 0, 1, 0),
    ("px", 7), ("px", 1), ("use", 1, 0), ("fin", 1), ("ex0", 1), ("ag", 0, 1, 4, 1),
    ("ag", 0, 0, 3, 0), ("px", 3), ("ag", 1, 1, 1, 1), ("fin", 0), ("ex0", 0), ("use", 0, 2),
    ("ag", 1, 0, 2, 1), ("ag", 1, 1, 1, 0), ("ag", 0, 1, 3, 0), ("ex1", 1), ("use", 1, 7),
    ("ag", 1, 0, 2, 0), ("px", 4), ("pk", 0), ("ex1", 0), ("ag", 1, 1, 2, 1), ("pk", 1),
    ("ag", 1, 0, 3, 1), ("ag", 1, 0, 3, 0), ("ag", 1, 1, 2, 0), ("ag", 0, 0, 4, 0),
    ("use", 1, 6), ("ag", 1, 1, 3, 1), ("use", 0, 3), ("ag", 1, 1, 3, 0), ("use", 0, 5),
    ("use", 1, 1), ("ag", 1, 0, 4, 0), ("use", 0, 1), ("ag", 1, 1, 4, 1), ("use", 1, 5),
    ("use", 0, 4), ("use", 1, 3), ("use", 1, 2),
)


def column_index(col, slot):
    me = lax.axis_index("fsdp")
    x = me % 2
    return lax.rem(me // 2 + slot, NZ) * 2 + (x if col == 0 else 1 - x)


def columns_of(ref, col, slot, rows, part=None):
    start = column_index(col, slot) * rows
    if part is not None:
        rows = rows // 2
        start = start + part * rows
    return ref.at[:, pl.ds(pl.multiple_of(start, rows), rows)]


def back_product(cot, block):
    return lax.dot_general(
        cot, block, (((1,), (1,)), ((), ())), preferred_element_type=F32
    ).astype(BF)


def kernel(
    act_h, w_h, cot_h, first_h, second_h, partner_h,
    kvacc, xga, xgb, xgc, kvc, first_new, second_new, stepped, final, wg, aoth, ccat,
    px_out, pk_out, pk_acc, acat, mom, rs_in, rs_out, gbuf, inbox_a, inbox_b, outbox, partner_s,
    load_sem, act_sem, x_send, x_recv, wx_send, wx_recv, ag_send, ag_recv,
    rs_send, rs_recv, ex_send, ex_recv, px_send, px_recv, pk_send, pk_recv,
):
    rep = lax.axis_index("rep")
    me = lax.axis_index("fsdp")
    inbox = (inbox_a, inbox_b)
    n_rep = inbox_a.shape[0]
    tok = cot_h.shape[0]
    rows, cols = w_h.shape
    half = cols // 2
    low_rows, high_rows = pl.ds(0, rows // 2), pl.ds(rows // 2, rows // 2)
    z, xl = me // 2, me % 2
    up = (rep, lax.rem(z + 1, NZ) * 2 + xl)
    down = (rep, lax.rem(z + NZ - 1, NZ) * 2 + xl)
    side = (rep, z * 2 + 1 - xl)
    ring = (up, down)

    def remote(src, dst, send, recv, target):
        return pltpu.make_async_remote_copy(
            src_ref=src, dst_ref=dst, send_sem=send, recv_sem=recv,
            device_id=target, device_id_type=MESH,
        )

    loads = {
        "cot": pltpu.make_async_copy(cot_h, ccat.at[pl.ds(0, tok)], load_sem.at[0]),
        "w": pltpu.make_async_copy(w_h, wg.at[0, 0], load_sem.at[1]),
        "first": pltpu.make_async_copy(first_h, mom.at[0], load_sem.at[2]),
        "second": pltpu.make_async_copy(second_h, mom.at[1], load_sem.at[3]),
        "partner": pltpu.make_async_copy(partner_h, partner_s, load_sem.at[4]),
    }
    for slot in range(NZ):
        loads[0, slot] = pltpu.make_async_copy(
            columns_of(act_h, 0, slot, rows), acat.at[slot, pl.ds(0, tok)], act_sem.at[0, slot]
        )
        loads[1, slot] = pltpu.make_async_copy(
            columns_of(act_h, 1, slot, rows, 0), aoth.at[slot], act_sem.at[1, slot]
        )
    waited = set()

    def loaded(key):
        if key not in waited:
            waited.add(key)
            loads[key].wait()

    copies = {
        ("xs", "cot"): remote(
            cot_h, ccat.at[pl.ds(tok, tok)], x_send.at[NZ], x_recv.at[NZ], side
        ),
        ("wxB",): remote(
            w_h.at[low_rows], wg.at[1, 0, low_rows], wx_send.at[0], wx_recv.at[0], side
        ),
    }
    for slot in range(NZ):
        copies["xs", slot] = remote(
            columns_of(act_h, 1, slot, rows), acat.at[slot, pl.ds(tok, tok)],
            x_send.at[slot], x_recv.at[slot], side,
        )
        copies["px", slot] = remote(
            px_out.at[slot], xgc.at[slot], px_send.at[slot], px_recv.at[slot], side
        )
    for part in range(2):
        span = (slice(None), pl.ds(part * half, half))
        copies["pk", part] = remote(
            pk_out.at[span], kvc.at[span], pk_send.at[part], pk_recv.at[part], side
        )

    def gather(col, direction, hop, part):
        length = rows // 2 if col == 0 else rows // 4
        span = pl.ds(part * length, length)
        if direction == 0:
            src, dst = (NZ - hop + 1) % NZ, NZ - hop
        else:
            src, dst = hop - 1, hop
        source = w_h.at[span] if (col == 0 and hop == 1) else wg.at[col, src, span]
        sems = (col, direction, hop - 1, part)
        return remote(
            source, wg.at[col, dst, span], ag_send.at[sems], ag_recv.at[sems], ring[direction]
        )

    def reduce_copy(direction, step, part):
        span = (direction, step, slice(None), pl.ds(part * half, half))
        return remote(
            rs_out.at[span], rs_in.at[span],
            rs_send.at[direction, step, part], rs_recv.at[direction, step, part],
            ring[direction],
        )

    for direction in range(2):
        for hop in range(1, HOPS + 1):
            for col in range(2):
                for part in range(2):
                    if hop < HOPS or part == direction:
                        token = ("ag", col, direction, hop, part)
                        copies[token] = gather(*token[1:])
        for step in range(HOPS):
            for part in range(2):
                if step > 0 or part == direction:
                    copies["rs", direction, step, part] = reduce_copy(direction, step, part)

    def exchange(phase, part):
        out = []
        for k in range(1, n_rep):
            peer = lax.rem(rep + k, n_rep)
            src = (stepped, outbox)[phase].at[part, peer]
            dst = final.at[part, rep] if phase else inbox[part].at[rep]
            out.append(
                remote(
                    src, dst,
                    ex_send.at[phase, part, k], ex_recv.at[phase, part, k], (peer, me),
                )
            )
        return out

    ex = {(phase, part): exchange(phase, part) for phase in range(2) for part in range(2)}

    def arrived(key):
        if key not in waited:
            waited.add(key)
            copies[key].wait_recv()

    def block_arrived(col, slot, parts=(0, 1)):
        for part in parts:
            if slot == 0:
                if col == 1:
                    arrived(("wxB",))
            elif slot == HOPS:
                arrived(("ag", col, part, HOPS, part))
            elif slot > HOPS:
                arrived(("ag", col, 0, NZ - slot, part))
            else:
                arrived(("ag", col, 1, slot, part))

    used = []

    def use_block(col, slot):
        block_arrived(col, slot)
        if col == 0 and slot == 0:
            loaded("w")
        loaded("cot")
        loaded((col, slot))
        if col == 0:
            tokens, block = acat[slot, pl.ds(0, tok)], wg[0, slot]
        else:
            tokens, block = aoth[slot], wg[1, slot, low_rows]
        term = jnp.dot(tokens, block, preferred_element_type=F32)
        if used:
            kvacc[...] += term
        else:
            kvacc[...] = term
        used.append((col, slot))
        (xga, xgb)[col][slot] = back_product(ccat[pl.ds(0, tok)], block)

    sided = []

    def side_products(slot):
        block_arrived(0, slot, (1,))
        arrived(("xs", "cot"))
        arrived(("xs", slot))
        if slot == 0:
            loaded("w")
        block = wg[0, slot, high_rows]
        px_out[slot] = back_product(ccat[pl.ds(tok, tok)], block)
        copies["px", slot].start()
        term = jnp.dot(acat[slot, pl.ds(tok, tok), high_rows], block, preferred_element_type=F32)
        if sided:
            pk_acc[...] += term
        else:
            pk_acc[...] = term
        sided.append(slot)

    def side_sum(part):
        span = pl.ds(part * half, half)
        pk_out[:, span] = pk_acc[:, span].astype(BF)
        copies["pk", part].start()

    def product(slot):
        arrived(("xs", "cot"))
        arrived(("xs", slot))
        loaded("cot")
        loaded((0, slot))
        gbuf[slot] = lax.dot_general(
            acat[slot], ccat[...], (((0,), (0,)), ((), ())), preferred_element_type=F32
        )

    def reduce_send(direction, step, part):
        span = pl.ds(part * half, half)
        slot = HOPS - step if direction == 0 else HOPS + step
        value = gbuf[slot, :, span]
        if ("rs", direction, step - 1, part) in copies:
            arrived(("rs", direction, step - 1, part))
            value = value + rs_in[direction, step - 1, :, span].astype(F32)
        rs_out[direction, step, :, span] = value.astype(BF)
        copies["rs", direction, step, part].start()

    def finish(part):
        span = pl.ds(part * half, half)
        for name in ("first", "second", "w"):
            loaded(name)
        grad = gbuf[0, :, span]
        for direction in range(2):
            arrived(("rs", direction, HOPS - 1, part))
            grad = grad + rs_in[direction, HOPS - 1, :, span].astype(F32)
        new_a = beta_one * mom[0, :, span] + (1.0 - beta_one) * grad
        new_b = beta_two * mom[1, :, span] + (1.0 - beta_two) * grad * grad
        first_new[:, span] = new_a
        second_new[:, span] = new_b
        old = wg[0, 0, :, span].astype(F32)
        update = new_a / corr_one / (jnp.sqrt(new_b / corr_two) + adam_eps) + weight_decay * old
        stepped[part] = (old - learn_rate * update).astype(BF).reshape(stepped.shape[1:])

    def exchange_first(part):
        for copy in ex[0, part]:
            copy.start()
        inbox[part][rep] = stepped[part, rep]

    def exchange_second(part):
        loaded("partner")
        for copy in ex[0, part]:
            copy.wait_recv()
        for j in range(n_rep):
            outbox[part, j] = inbox[part][partner_s[j]]
        for copy in ex[1, part]:
            copy.start()
        final[part, rep] = outbox[part, rep]

    barrier = pltpu.get_barrier_semaphore()
    others = [(lax.rem(rep + k, n_rep), me) for k in range(1, n_rep)]
    for device in (up, down, side, *others):
        pl.semaphore_signal(barrier, inc=1, device_id=device, device_id_type=MESH)
    loads["cot"].start()
    loads["w"].start()
    for slot in (0, 7, 1, 4, 3, 5, 2, 6):
        loads[0, slot].start()
    pl.semaphore_wait(barrier, 3 + n_rep - 1)

    actions = {
        "use": use_block, "g": product, "rs": reduce_send, "fin": finish,
        "ex0": exchange_first, "ex1": exchange_second, "px": side_products, "pk": side_sum,
    }
    for position, token in enumerate(SCHEDULE):
        if position == LATE_LOADS:
            for slot in range(NZ):
                loads[1, slot].start()
            for name in ("first", "second", "partner"):
                loads[name].start()
        name = token[0]
        if name in actions:
            actions[name](*token[1:])
            continue
        if name == "ag":
            _, col, direction, hop, part = token
            if hop > 1:
                arrived(("ag", col, direction, hop - 1, part))
            elif col == 1:
                arrived(("wxB",))
        copies[token].start()

    for key, copy in copies.items():
        arrived(key)
        copy.wait_send()
    for part in range(2):
        for copy in ex[1, part]:
            copy.wait_recv()
        for phase in range(2):
            for copy in ex[phase, part]:
                copy.wait_send()
    for key in loads:
        loaded(key)


LATE_LOADS = 16
LEFT = tuple(
    (col, slot)
    for slot in (0, 7, 1, 6, 2, 5, 3, 4)
    for col in range(2)
    if ("use", col, slot) not in SCHEDULE
)


def write_out(
    kvacc, xga, xgb, xgc, kvc, first_new, second_new, stepped, final, wg, aoth, ccat, mix_h,
    kv_h, xg_h, nw_h, nf_h, ns_h,
    kvb, xgl, nwv, mix_s, xg_sem, sem,
):
    tok = kvb.shape[0]
    rows, cols = nwv.shape
    half = cols // 2
    mix_load = pltpu.make_async_copy(mix_h, mix_s, sem.at[4])
    mix_load.start()
    copies = [
        pltpu.make_async_copy(first_new, nf_h, sem.at[0]),
        pltpu.make_async_copy(second_new, ns_h, sem.at[1]),
    ]
    for slot in range(NZ):
        blocks = [(xga, 0, None, 0), (xgc, 1, 1, 2)]
        if (1, slot) not in LEFT:
            blocks.append((xgb, 1, 0, 1))
        for source, col, part, sem_row in blocks:
            copies.append(
                pltpu.make_async_copy(
                    source.at[slot],
                    columns_of(xg_h, col, slot, rows, part),
                    xg_sem.at[sem_row, slot],
                )
            )
    for copy in copies:
        copy.start()
    total = kvacc[...] + kvc[...].astype(F32)
    for i, (col, slot) in enumerate(LEFT):
        block = wg[col, slot, pl.ds(0, rows // 2)]
        total = total + jnp.dot(aoth[slot], block, preferred_element_type=F32)
        xgl[i] = back_product(ccat[pl.ds(0, tok)], block)
        copy = pltpu.make_async_copy(
            xgl.at[i], columns_of(xg_h, col, slot, rows, 0), xg_sem.at[col, slot]
        )
        copy.start()
        copies.append(copy)
    kvb[...] = total.astype(BF)
    copies.append(pltpu.make_async_copy(kvb, kv_h, sem.at[2]))
    copies[-1].start()
    mix_load.wait()
    mixing = mix_s[lax.axis_index("rep")].astype(F32) / mix_denom
    for part in range(2):
        nwv[:, pl.ds(part * half, half)] = (
            ((1.0 - mixing) * stepped[part].astype(F32) + mixing * final[part].astype(F32))
            .astype(BF)
            .reshape(rows, half)
        )
    copies.append(pltpu.make_async_copy(nwv, nw_h, sem.at[3]))
    copies[-1].start()
    for copy in copies:
        copy.wait()


def per_device(
    activations, kv_weight, kv_cotangent, first_moment, second_moment, partner, mix_numerator
):
    act, weights, cot = activations[0], kv_weight[0], kv_cotangent[0]
    tok, width = act.shape
    rows, cols = weights.shape
    n_rep = partner.shape[0]
    chunks = (2, n_rep, rows // n_rep, cols // 2)
    dma = pltpu.SemaphoreType.DMA
    hbm = pl.BlockSpec(memory_space=pltpu.HBM)
    vmem = pl.BlockSpec(memory_space=pltpu.VMEM)

    def in_hbm(x):
        return pltpu.with_memory_space_constraint(x, pltpu.HBM)

    held = pl.pallas_call(
        kernel,
        out_shape=(
            pltpu.VMEM((tok, cols), F32),
            pltpu.VMEM((NZ, tok, rows), BF),
            pltpu.VMEM((NZ, tok, rows // 2), BF),
            pltpu.VMEM((NZ, tok, rows // 2), BF),
            pltpu.VMEM((tok, cols), BF),
            pltpu.VMEM((rows, cols), F32),
            pltpu.VMEM((rows, cols), F32),
            pltpu.VMEM(chunks, BF),
            pltpu.VMEM(chunks, BF),
            pltpu.VMEM((2, NZ, rows, cols), BF),
            pltpu.VMEM((NZ, tok, rows // 2), BF),
            pltpu.VMEM((2 * tok, cols), BF),
        ),
        in_specs=[hbm] * 6,
        out_specs=[vmem] * 12,
        scratch_shapes=[
            pltpu.VMEM((NZ, tok, rows // 2), BF),
            pltpu.VMEM((tok, cols), BF),
            pltpu.VMEM((tok, cols), F32),
            pltpu.VMEM((NZ, 2 * tok, rows), BF),
            pltpu.VMEM((2, rows, cols), F32),
            pltpu.VMEM((2, HOPS, rows, cols), BF),
            pltpu.VMEM((2, HOPS, rows, cols), BF),
            pltpu.VMEM((NZ, rows, cols), F32),
            pltpu.VMEM(chunks[1:], BF),
            pltpu.VMEM(chunks[1:], BF),
            pltpu.VMEM(chunks, BF),
            pltpu.SMEM((n_rep,), jnp.int32),
            dma((5,)),
            dma((2, NZ)),
            dma((NZ + 1,)),
            dma((NZ + 1,)),
            dma((1,)),
            dma((1,)),
            dma((2, 2, HOPS, 2)),
            dma((2, 2, HOPS, 2)),
            dma((2, HOPS, 2)),
            dma((2, HOPS, 2)),
            dma((2, 2, n_rep)),
            dma((2, 2, n_rep)),
            dma((NZ,)),
            dma((NZ,)),
            dma((2,)),
            dma((2,)),
        ],
        name="step",
        compiler_params=pltpu.CompilerParams(
            collective_id=0, has_side_effects=True, vmem_limit_bytes=32 << 20
        ),
    )(*(in_hbm(x) for x in (act, weights, cot, first_moment[0], second_moment[0], partner)))
    outs = pl.pallas_call(
        write_out,
        out_shape=(
            jax.ShapeDtypeStruct((tok, cols), BF),
            jax.ShapeDtypeStruct((tok, width), BF),
            jax.ShapeDtypeStruct((rows, cols), BF),
            jax.ShapeDtypeStruct((rows, cols), F32),
            jax.ShapeDtypeStruct((rows, cols), F32),
        ),
        in_specs=[vmem] * 12 + [hbm],
        out_specs=[hbm] * 5,
        scratch_shapes=[
            pltpu.VMEM((tok, cols), BF),
            pltpu.VMEM((len(LEFT), tok, rows // 2), BF),
            pltpu.VMEM((rows, cols), BF),
            pltpu.SMEM((n_rep,), jnp.int32),
            dma((3, NZ)),
            dma((5,)),
        ],
        name="write_out",
        compiler_params=pltpu.CompilerParams(vmem_limit_bytes=8 << 20),
    )(*held, in_hbm(mix_numerator))
    return tuple(out[None] for out in outs)


def solution(mesh):
    split = P("rep", "fsdp", None)
    return jax.shard_map(
        per_device,
        mesh=mesh,
        in_specs=(split,) * 5 + (P(), P()),
        out_specs=(split,) * 5,
        check_vma=False,
    )
```

```python
import jax
import jax.numpy as jnp
from jax import lax
from jax.experimental import pallas as pl
from jax.experimental.pallas import tpu as pltpu
from jax.sharding import PartitionSpec as P

beta_one = 0.9
beta_two = 0.999
learn_rate = 0.02
weight_decay = 0.1
adam_eps = 1e-08
corr_one = 1.0 - beta_one**10
corr_two = 1.0 - beta_two**10
mix_denom = 64.0

MESH = pl.DeviceIdType.MESH
BF = jnp.bfloat16
F32 = jnp.float32
NZ = 8
HOPS = NZ // 2

SCHEDULE = (
    ("xs", "cot"), ("xs", 4), ("xs", 3), ("ag", 0, 1, 1, 0), ("ag", 0, 0, 1, 1),
    ("ag", 0, 0, 1, 0), ("ag", 0, 1, 1, 1), ("xs", 5), ("ag", 0, 0, 2, 1), ("xs", 2), ("xs", 1),
    ("xs", 6), ("ag", 0, 1, 2, 0), ("ag", 0, 1, 2, 1), ("ag", 0, 0, 2, 0), ("xs", 0),
    ("ag", 0, 0, 3, 1), ("g", 4), ("rs", 1, 0, 1), ("ag", 0, 1, 3, 1), ("rs", 0, 0, 0), ("g", 5),
    ("xs", 7), ("rs", 1, 1, 1), ("wxB",), ("g", 3), ("rs", 0, 1, 1), ("use", 0, 7),
    ("rs", 1, 1, 0), ("rs", 0, 1, 0), ("use", 0, 0), ("g", 2), ("g", 1), ("g", 6),
    ("rs", 0, 2, 1), ("rs", 1, 2, 1), ("px", 6), ("px", 5), ("rs", 1, 2, 0), ("rs", 0, 2, 0),
    ("g", 7), ("g", 0), ("rs", 0, 3, 1), ("px", 2), ("rs", 1, 3, 1), ("use", 0, 6),
    ("rs", 1, 3, 0), ("px", 0), ("rs", 0, 3, 0), ("ag", 1, 0, 1, 1), ("ag", 1, 0, 1, 0),
    ("px", 7), ("px", 1), ("use", 1, 0), ("fin", 1), ("ex0", 1), ("ag", 0, 1, 4, 1),
    ("ag", 0, 0, 3, 0), ("px", 3), ("ag", 1, 1, 1, 1), ("fin", 0), ("ex0", 0), ("use", 0, 2),
    ("ag", 1, 0, 2, 1), ("ag", 1, 1, 1, 0), ("ag", 0, 1, 3, 0), ("ex1", 1), ("use", 1, 7),
    ("ag", 1, 0, 2, 0), ("px", 4), ("pk", 0), ("ex1", 0), ("ag", 1, 1, 2, 1), ("pk", 1),
    ("ag", 1, 0, 3, 1), ("ag", 1, 0, 3, 0), ("ag", 1, 1, 2, 0), ("ag", 0, 0, 4, 0),
    ("use", 1, 6), ("ag", 1, 1, 3, 1), ("use", 0, 3), ("ag", 1, 1, 3, 0), ("use", 0, 5),
    ("use", 1, 1), ("use", 0, 1), ("ag", 1, 1, 4, 1), ("ag", 1, 0, 4, 0), ("use", 1, 2),
    ("exf",), ("use", 1, 5), ("use", 0, 4), ("use", 1, 3),
)


def column_index(col, slot):
    me = lax.axis_index("fsdp")
    x = me % 2
    return lax.rem(me // 2 + slot, NZ) * 2 + (x if col == 0 else 1 - x)


def columns_of(ref, col, slot, rows, part=None):
    start = column_index(col, slot) * rows
    if part is not None:
        rows = rows // 2
        start = start + part * rows
    return ref.at[:, pl.ds(pl.multiple_of(start, rows), rows)]


def back_product(cot, block):
    return lax.dot_general(
        cot, block, (((1,), (1,)), ((), ())), preferred_element_type=F32
    ).astype(BF)


def kernel(
    act_h, w_h, cot_h, first_h, second_h, partner_h, mix_h,
    kvacc, xga, xgb, xgc, kvc, first_new, second_new, nwv, wg, aoth, ccat,
    stepped, final, px_out, pk_out, pk_acc, acat, mom, rs_in, rs_out, gbuf, inbox_a, inbox_b, outbox, partner_s, mix_s,
    load_sem, act_sem, x_send, x_recv, wx_send, wx_recv, ag_send, ag_recv,
    rs_send, rs_recv, ex_send, ex_recv, px_send, px_recv, pk_send, pk_recv,
):
    rep = lax.axis_index("rep")
    me = lax.axis_index("fsdp")
    inbox = (inbox_a, inbox_b)
    n_rep = inbox_a.shape[0]
    tok = cot_h.shape[0]
    rows, cols = w_h.shape
    half = cols // 2
    low_rows, high_rows = pl.ds(0, rows // 2), pl.ds(rows // 2, rows // 2)
    z, xl = me // 2, me % 2
    up = (rep, lax.rem(z + 1, NZ) * 2 + xl)
    down = (rep, lax.rem(z + NZ - 1, NZ) * 2 + xl)
    side = (rep, z * 2 + 1 - xl)
    ring = (up, down)

    def remote(src, dst, send, recv, target):
        return pltpu.make_async_remote_copy(
            src_ref=src, dst_ref=dst, send_sem=send, recv_sem=recv,
            device_id=target, device_id_type=MESH,
        )

    loads = {
        "cot": pltpu.make_async_copy(cot_h, ccat.at[pl.ds(0, tok)], load_sem.at[0]),
        "w": pltpu.make_async_copy(w_h, wg.at[0, 0], load_sem.at[1]),
        "first": pltpu.make_async_copy(first_h, mom.at[0], load_sem.at[2]),
        "second": pltpu.make_async_copy(second_h, mom.at[1], load_sem.at[3]),
        "partner": pltpu.make_async_copy(partner_h, partner_s, load_sem.at[4]),
        "mix": pltpu.make_async_copy(mix_h, mix_s, load_sem.at[5]),
    }
    for slot in range(NZ):
        loads[0, slot] = pltpu.make_async_copy(
            columns_of(act_h, 0, slot, rows), acat.at[slot, pl.ds(0, tok)], act_sem.at[0, slot]
        )
        loads[1, slot] = pltpu.make_async_copy(
            columns_of(act_h, 1, slot, rows, 0), aoth.at[slot], act_sem.at[1, slot]
        )
    waited = set()

    def loaded(key):
        if key not in waited:
            waited.add(key)
            loads[key].wait()

    copies = {
        ("xs", "cot"): remote(
            cot_h, ccat.at[pl.ds(tok, tok)], x_send.at[NZ], x_recv.at[NZ], side
        ),
        ("wxB",): remote(
            w_h.at[low_rows], wg.at[1, 0, low_rows], wx_send.at[0], wx_recv.at[0], side
        ),
    }
    for slot in range(NZ):
        copies["xs", slot] = remote(
            columns_of(act_h, 1, slot, rows), acat.at[slot, pl.ds(tok, tok)],
            x_send.at[slot], x_recv.at[slot], side,
        )
        copies["px", slot] = remote(
            px_out.at[slot], xgc.at[slot], px_send.at[slot], px_recv.at[slot], side
        )
    for part in range(2):
        span = (slice(None), pl.ds(part * half, half))
        copies["pk", part] = remote(
            pk_out.at[span], kvc.at[span], pk_send.at[part], pk_recv.at[part], side
        )

    def gather(col, direction, hop, part):
        length = rows // 2 if col == 0 else rows // 4
        span = pl.ds(part * length, length)
        if direction == 0:
            src, dst = (NZ - hop + 1) % NZ, NZ - hop
        else:
            src, dst = hop - 1, hop
        source = w_h.at[span] if (col == 0 and hop == 1) else wg.at[col, src, span]
        sems = (col, direction, hop - 1, part)
        return remote(
            source, wg.at[col, dst, span], ag_send.at[sems], ag_recv.at[sems], ring[direction]
        )

    def reduce_copy(direction, step, part):
        span = (direction, step, slice(None), pl.ds(part * half, half))
        return remote(
            rs_out.at[span], rs_in.at[span],
            rs_send.at[direction, step, part], rs_recv.at[direction, step, part],
            ring[direction],
        )

    for direction in range(2):
        for hop in range(1, HOPS + 1):
            for col in range(2):
                for part in range(2):
                    if hop < HOPS or part == direction:
                        token = ("ag", col, direction, hop, part)
                        copies[token] = gather(*token[1:])
        for step in range(HOPS):
            for part in range(2):
                if step > 0 or part == direction:
                    copies["rs", direction, step, part] = reduce_copy(direction, step, part)

    def exchange(phase, part):
        out = []
        for k in range(1, n_rep):
            peer = lax.rem(rep + k, n_rep)
            src = (stepped, outbox)[phase].at[part, peer]
            dst = final.at[part, rep] if phase else inbox[part].at[rep]
            out.append(
                remote(
                    src, dst,
                    ex_send.at[phase, part, k], ex_recv.at[phase, part, k], (peer, me),
                )
            )
        return out

    ex = {(phase, part): exchange(phase, part) for phase in range(2) for part in range(2)}

    def arrived(key):
        if key not in waited:
            waited.add(key)
            copies[key].wait_recv()

    def block_arrived(col, slot, parts=(0, 1)):
        for part in parts:
            if slot == 0:
                if col == 1:
                    arrived(("wxB",))
            elif slot == HOPS:
                arrived(("ag", col, part, HOPS, part))
            elif slot > HOPS:
                arrived(("ag", col, 0, NZ - slot, part))
            else:
                arrived(("ag", col, 1, slot, part))

    used = []

    def use_block(col, slot):
        block_arrived(col, slot)
        if col == 0 and slot == 0:
            loaded("w")
        loaded("cot")
        loaded((col, slot))
        if col == 0:
            tokens, block = acat[slot, pl.ds(0, tok)], wg[0, slot]
        else:
            tokens, block = aoth[slot], wg[1, slot, low_rows]
        term = jnp.dot(tokens, block, preferred_element_type=F32)
        if used:
            kvacc[...] += term
        else:
            kvacc[...] = term
        used.append((col, slot))
        (xga, xgb)[col][slot] = back_product(ccat[pl.ds(0, tok)], block)

    sided = []

    def side_products(slot):
        block_arrived(0, slot, (1,))
        arrived(("xs", "cot"))
        arrived(("xs", slot))
        if slot == 0:
            loaded("w")
        block = wg[0, slot, high_rows]
        px_out[slot] = back_product(ccat[pl.ds(tok, tok)], block)
        copies["px", slot].start()
        term = jnp.dot(acat[slot, pl.ds(tok, tok), high_rows], block, preferred_element_type=F32)
        if sided:
            pk_acc[...] += term
        else:
            pk_acc[...] = term
        sided.append(slot)

    def side_sum(part):
        span = pl.ds(part * half, half)
        pk_out[:, span] = pk_acc[:, span].astype(BF)
        copies["pk", part].start()

    def product(slot):
        arrived(("xs", "cot"))
        arrived(("xs", slot))
        loaded("cot")
        loaded((0, slot))
        gbuf[slot] = lax.dot_general(
            acat[slot], ccat[...], (((0,), (0,)), ((), ())), preferred_element_type=F32
        )

    def reduce_send(direction, step, part):
        span = pl.ds(part * half, half)
        slot = HOPS - step if direction == 0 else HOPS + step
        value = gbuf[slot, :, span]
        if ("rs", direction, step - 1, part) in copies:
            arrived(("rs", direction, step - 1, part))
            value = value + rs_in[direction, step - 1, :, span].astype(F32)
        rs_out[direction, step, :, span] = value.astype(BF)
        copies["rs", direction, step, part].start()

    def finish(part):
        span = pl.ds(part * half, half)
        for name in ("first", "second", "w"):
            loaded(name)
        grad = gbuf[0, :, span]
        for direction in range(2):
            arrived(("rs", direction, HOPS - 1, part))
            grad = grad + rs_in[direction, HOPS - 1, :, span].astype(F32)
        new_a = beta_one * mom[0, :, span] + (1.0 - beta_one) * grad
        new_b = beta_two * mom[1, :, span] + (1.0 - beta_two) * grad * grad
        first_new[:, span] = new_a
        second_new[:, span] = new_b
        old = wg[0, 0, :, span].astype(F32)
        update = new_a / corr_one / (jnp.sqrt(new_b / corr_two) + adam_eps) + weight_decay * old
        stepped[part] = (old - learn_rate * update).astype(BF).reshape(stepped.shape[1:])

    def exchange_first(part):
        for copy in ex[0, part]:
            copy.start()
        inbox[part][rep] = stepped[part, rep]

    def exchange_second(part):
        loaded("partner")
        for copy in ex[0, part]:
            copy.wait_recv()
        for j in range(n_rep):
            outbox[part, j] = inbox[part][partner_s[j]]
        for copy in ex[1, part]:
            copy.start()
        final[part, rep] = outbox[part, rep]

    def average():
        loaded("mix")
        mixing = mix_s[rep].astype(F32) / mix_denom
        for part in range(2):
            for copy in ex[1, part]:
                copy.wait_recv()
            own, other = stepped[part].astype(F32), final[part].astype(F32)
            nwv[:, pl.ds(part * half, half)] = (
                ((1.0 - mixing) * own + mixing * other).astype(BF).reshape(rows, half)
            )

    barrier = pltpu.get_barrier_semaphore()
    others = [(lax.rem(rep + k, n_rep), me) for k in range(1, n_rep)]
    for device in (up, down, side, *others):
        pl.semaphore_signal(barrier, inc=1, device_id=device, device_id_type=MESH)
    loads["cot"].start()
    loads["w"].start()
    for slot in (0, 7, 1, 4, 3, 5, 2, 6):
        loads[0, slot].start()
    pl.semaphore_wait(barrier, 3 + n_rep - 1)

    actions = {
        "use": use_block, "g": product, "rs": reduce_send, "fin": finish,
        "ex0": exchange_first, "ex1": exchange_second, "px": side_products, "pk": side_sum, "exf": average,
    }
    for position, token in enumerate(SCHEDULE):
        if position == LATE_LOADS:
            for slot in range(NZ):
                loads[1, slot].start()
            for name in ("first", "second", "partner", "mix"):
                loads[name].start()
        name = token[0]
        if name in actions:
            actions[name](*token[1:])
            continue
        if name == "ag":
            _, col, direction, hop, part = token
            if hop > 1:
                arrived(("ag", col, direction, hop - 1, part))
            elif col == 1:
                arrived(("wxB",))
        copies[token].start()

    for key in loads:
        loaded(key)
    for phase in range(2):
        for part in range(2):
            for copy in ex[phase, part]:
                copy.wait_send()
    sent = [token for token in SCHEDULE if token in copies]
    for token in sent[:-LAST]:
        copies[token].wait_send()
    for token in sent:
        arrived(token)
    for token in sent[-LAST:]:
        copies[token].wait_send()


LAST = 8
LATE_LOADS = 16
LEFT = tuple(
    (col, slot)
    for slot in (0, 7, 1, 6, 2, 5, 3, 4)
    for col in range(2)
    if ("use", col, slot) not in SCHEDULE
)


def write_out(
    kvacc, xga, xgb, xgc, kvc, first_new, second_new, nwv, wg, aoth, ccat,
    kv_h, xg_h, nw_h, nf_h, ns_h,
    kvb, xgl, xg_sem, sem,
):
    tok = kvb.shape[0]
    rows = nwv.shape[0]
    copies = [
        pltpu.make_async_copy(first_new, nf_h, sem.at[0]),
        pltpu.make_async_copy(second_new, ns_h, sem.at[1]),
        pltpu.make_async_copy(nwv, nw_h, sem.at[3]),
    ]
    for slot in range(NZ):
        blocks = [(xga, 0, None, 0), (xgc, 1, 1, 2)]
        if (1, slot) not in LEFT:
            blocks.append((xgb, 1, 0, 1))
        for source, col, part, sem_row in blocks:
            copies.append(
                pltpu.make_async_copy(
                    source.at[slot],
                    columns_of(xg_h, col, slot, rows, part),
                    xg_sem.at[sem_row, slot],
                )
            )
    for copy in copies:
        copy.start()
    total = kvacc[...] + kvc[...].astype(F32)
    for i, (col, slot) in enumerate(LEFT):
        block = wg[col, slot, pl.ds(0, rows // 2)]
        total = total + jnp.dot(aoth[slot], block, preferred_element_type=F32)
        xgl[i] = back_product(ccat[pl.ds(0, tok)], block)
        copy = pltpu.make_async_copy(
            xgl.at[i], columns_of(xg_h, col, slot, rows, 0), xg_sem.at[col, slot]
        )
        copy.start()
        copies.append(copy)
    kvb[...] = total.astype(BF)
    copies.append(pltpu.make_async_copy(kvb, kv_h, sem.at[2]))
    copies[-1].start()
    for copy in copies:
        copy.wait()


def per_device(
    activations, kv_weight, kv_cotangent, first_moment, second_moment, partner, mix_numerator
):
    act, weights, cot = activations[0], kv_weight[0], kv_cotangent[0]
    tok, width = act.shape
    rows, cols = weights.shape
    n_rep = partner.shape[0]
    chunks = (2, n_rep, rows // n_rep, cols // 2)
    dma = pltpu.SemaphoreType.DMA
    hbm = pl.BlockSpec(memory_space=pltpu.HBM)
    vmem = pl.BlockSpec(memory_space=pltpu.VMEM)

    def in_hbm(x):
        return pltpu.with_memory_space_constraint(x, pltpu.HBM)

    held = pl.pallas_call(
        kernel,
        out_shape=(
            pltpu.VMEM((tok, cols), F32),
            pltpu.VMEM((NZ, tok, rows), BF),
            pltpu.VMEM((NZ, tok, rows // 2), BF),
            pltpu.VMEM((NZ, tok, rows // 2), BF),
            pltpu.VMEM((tok, cols), BF),
            pltpu.VMEM((rows, cols), F32),
            pltpu.VMEM((rows, cols), F32),
            pltpu.VMEM((rows, cols), BF),
            pltpu.VMEM((2, NZ, rows, cols), BF),
            pltpu.VMEM((NZ, tok, rows // 2), BF),
            pltpu.VMEM((2 * tok, cols), BF),
        ),
        in_specs=[hbm] * 7,
        out_specs=[vmem] * 11,
        scratch_shapes=[
            pltpu.VMEM(chunks, BF),
            pltpu.VMEM(chunks, BF),
            pltpu.VMEM((NZ, tok, rows // 2), BF),
            pltpu.VMEM((tok, cols), BF),
            pltpu.VMEM((tok, cols), F32),
            pltpu.VMEM((NZ, 2 * tok, rows), BF),
            pltpu.VMEM((2, rows, cols), F32),
            pltpu.VMEM((2, HOPS, rows, cols), BF),
            pltpu.VMEM((2, HOPS, rows, cols), BF),
            pltpu.VMEM((NZ, rows, cols), F32),
            pltpu.VMEM(chunks[1:], BF),
            pltpu.VMEM(chunks[1:], BF),
            pltpu.VMEM(chunks, BF),
            pltpu.SMEM((n_rep,), jnp.int32),
            pltpu.SMEM((n_rep,), jnp.int32),
            dma((6,)),
            dma((2, NZ)),
            dma((NZ + 1,)),
            dma((NZ + 1,)),
            dma((1,)),
            dma((1,)),
            dma((2, 2, HOPS, 2)),
            dma((2, 2, HOPS, 2)),
            dma((2, HOPS, 2)),
            dma((2, HOPS, 2)),
            dma((2, 2, n_rep)),
            dma((2, 2, n_rep)),
            dma((NZ,)),
            dma((NZ,)),
            dma((2,)),
            dma((2,)),
        ],
        name="step",
        compiler_params=pltpu.CompilerParams(
            collective_id=0, has_side_effects=True, vmem_limit_bytes=32 << 20
        ),
    )(
        *(
            in_hbm(x)
            for x in (act, weights, cot, first_moment[0], second_moment[0], partner, mix_numerator)
        )
    )
    outs = pl.pallas_call(
        write_out,
        out_shape=(
            jax.ShapeDtypeStruct((tok, cols), BF),
            jax.ShapeDtypeStruct((tok, width), BF),
            jax.ShapeDtypeStruct((rows, cols), BF),
            jax.ShapeDtypeStruct((rows, cols), F32),
            jax.ShapeDtypeStruct((rows, cols), F32),
        ),
        in_specs=[vmem] * 11,
        out_specs=[hbm] * 5,
        scratch_shapes=[
            pltpu.VMEM((tok, cols), BF),
            pltpu.VMEM((len(LEFT), tok, rows // 2), BF),
            dma((3, NZ)),
            dma((4,)),
        ],
        name="write_out",
        compiler_params=pltpu.CompilerParams(vmem_limit_bytes=8 << 20),
    )(*held)
    return tuple(out[None] for out in outs)


def solution(mesh):
    split = P("rep", "fsdp", None)
    return jax.shard_map(
        per_device,
        mesh=mesh,
        in_specs=(split,) * 5 + (P(), P()),
        out_specs=(split,) * 5,
        check_vma=False,
    )
```

```python
import jax
import jax.numpy as jnp
from jax import lax
from jax.experimental import pallas as pl
from jax.experimental.pallas import tpu as pltpu
from jax.sharding import PartitionSpec as P

beta_one = 0.9
beta_two = 0.999
learn_rate = 0.02
weight_decay = 0.1
adam_eps = 1e-08
corr_one = 1.0 - beta_one**10
corr_two = 1.0 - beta_two**10
mix_denom = 64.0

MESH = pl.DeviceIdType.MESH
BF = jnp.bfloat16
F32 = jnp.float32
NZ = 8
HOPS = NZ // 2

SCHEDULE = (
    ("xs", "cot"), ("ag", 0, 1, 1, 0), ("ag", 0, 0, 1, 1), ("ag", 0, 0, 1, 0),
    ("ag", 0, 1, 1, 1), ("xs", 4), ("xs", 3), ("xs", 5), ("ag", 0, 0, 2, 1), ("xs", 2),
    ("xs", 1), ("xs", 6), ("ag", 0, 1, 2, 0), ("ag", 0, 1, 2, 1), ("ag", 0, 0, 2, 0), ("xs", 0),
    ("ag", 0, 0, 3, 1), ("g", 4), ("rs", 1, 0, 1), ("ag", 0, 1, 3, 1), ("rs", 0, 0, 0), ("g", 5),
    ("xs", 7), ("rs", 1, 1, 1), ("wxB",), ("g", 3), ("rs", 0, 1, 1), ("use", 0, 7),
    ("rs", 1, 1, 0), ("rs", 0, 1, 0), ("use", 0, 0), ("g", 2), ("g", 1), ("g", 6),
    ("rs", 0, 2, 1), ("rs", 1, 2, 1), ("px", 6), ("px", 5), ("rs", 1, 2, 0), ("rs", 0, 2, 0),
    ("g", 7), ("g", 0), ("rs", 0, 3, 1), ("px", 2), ("rs", 1, 3, 1), ("use", 0, 6),
    ("rs", 1, 3, 0), ("px", 0), ("rs", 0, 3, 0), ("ag", 1, 0, 1, 1), ("ag", 1, 0, 1, 0),
    ("px", 7), ("px", 1), ("use", 1, 0), ("fin", 1), ("ex0", 1), ("ag", 0, 1, 4, 1),
    ("ag", 0, 0, 3, 0), ("px", 3), ("ag", 1, 1, 1, 1), ("fin", 0), ("ex0", 0), ("use", 0, 2),
    ("ag", 1, 0, 2, 1), ("ag", 1, 1, 1, 0), ("ag", 0, 1, 3, 0), ("ex1", 1), ("use", 1, 7),
    ("ag", 1, 0, 2, 0), ("px", 4), ("pk", 0), ("ex1", 0), ("ag", 1, 1, 2, 1), ("pk", 1),
    ("ag", 1, 0, 3, 1), ("ag", 1, 0, 3, 0), ("ag", 1, 1, 2, 0), ("ag", 0, 0, 4, 0),
    ("use", 1, 6), ("ag", 1, 1, 3, 1), ("use", 0, 3), ("ag", 1, 1, 3, 0), ("use", 0, 5),
    ("use", 1, 1), ("use", 0, 1), ("ag", 1, 1, 4, 1), ("ag", 1, 0, 4, 0), ("use", 1, 2),
    ("exf",), ("use", 1, 5), ("use", 0, 4), ("use", 1, 3),
)


def column_index(col, slot):
    me = lax.axis_index("fsdp")
    x = me % 2
    return lax.rem(me // 2 + slot, NZ) * 2 + (x if col == 0 else 1 - x)


def columns_of(ref, col, slot, rows, part=None):
    start = column_index(col, slot) * rows
    if part is not None:
        rows = rows // 2
        start = start + part * rows
    return ref.at[:, pl.ds(pl.multiple_of(start, rows), rows)]


def back_product(cot, block):
    return lax.dot_general(
        cot, block, (((1,), (1,)), ((), ())), preferred_element_type=F32
    ).astype(BF)


def kernel(
    act_h, w_h, cot_h, first_h, second_h, partner_h, mix_h,
    kvacc, xga, xgb, kvc, first_new, second_new, nwv, wg, aoth, ccat,
    stepped, final, px_out, pk_out, pk_acc, acat, mom, rs_in, rs_out, gbuf, inbox_a, inbox_b, outbox, partner_s, mix_s,
    load_sem, act_sem, x_send, x_recv, wx_send, wx_recv, ag_send, ag_recv,
    rs_send, rs_recv, ex_send, ex_recv, px_send, px_recv, pk_send, pk_recv,
):
    rep = lax.axis_index("rep")
    me = lax.axis_index("fsdp")
    inbox = (inbox_a, inbox_b)
    n_rep = inbox_a.shape[0]
    tok = cot_h.shape[0]
    rows, cols = w_h.shape
    half = cols // 2
    low_rows, high_rows = pl.ds(0, rows // 2), pl.ds(rows // 2, rows // 2)
    z, xl = me // 2, me % 2
    up = (rep, lax.rem(z + 1, NZ) * 2 + xl)
    down = (rep, lax.rem(z + NZ - 1, NZ) * 2 + xl)
    side = (rep, z * 2 + 1 - xl)
    ring = (up, down)

    def remote(src, dst, send, recv, target):
        return pltpu.make_async_remote_copy(
            src_ref=src, dst_ref=dst, send_sem=send, recv_sem=recv,
            device_id=target, device_id_type=MESH,
        )

    loads = {
        "cot": pltpu.make_async_copy(cot_h, ccat.at[pl.ds(0, tok)], load_sem.at[0]),
        "w": pltpu.make_async_copy(w_h, wg.at[0, 0], load_sem.at[1]),
        "first": pltpu.make_async_copy(first_h, mom.at[0], load_sem.at[2]),
        "second": pltpu.make_async_copy(second_h, mom.at[1], load_sem.at[3]),
        "partner": pltpu.make_async_copy(partner_h, partner_s, load_sem.at[4]),
        "mix": pltpu.make_async_copy(mix_h, mix_s, load_sem.at[5]),
    }
    for slot in range(NZ):
        loads[0, slot] = pltpu.make_async_copy(
            columns_of(act_h, 0, slot, rows), acat.at[slot, pl.ds(0, tok)], act_sem.at[0, slot]
        )
        loads[1, slot] = pltpu.make_async_copy(
            columns_of(act_h, 1, slot, rows), aoth.at[slot], act_sem.at[1, slot]
        )
    waited = set()

    def loaded(key):
        if key not in waited:
            waited.add(key)
            loads[key].wait()

    copies = {
        ("xs", "cot"): remote(
            cot_h, ccat.at[pl.ds(tok, tok)], x_send.at[NZ], x_recv.at[NZ], side
        ),
        ("wxB",): remote(
            w_h.at[low_rows], wg.at[1, 0, low_rows], wx_send.at[0], wx_recv.at[0], side
        ),
    }
    for slot in range(NZ):
        copies["xs", slot] = remote(
            aoth.at[slot], acat.at[slot, pl.ds(tok, tok)],
            x_send.at[slot], x_recv.at[slot], side,
        )
        copies["px", slot] = remote(
            px_out.at[slot], xgb.at[slot, :, high_rows], px_send.at[slot], px_recv.at[slot], side
        )
    for part in range(2):
        span = (slice(None), pl.ds(part * half, half))
        copies["pk", part] = remote(
            pk_out.at[span], kvc.at[span], pk_send.at[part], pk_recv.at[part], side
        )

    def gather(col, direction, hop, part):
        length = rows // 2 if col == 0 else rows // 4
        span = pl.ds(part * length, length)
        if direction == 0:
            src, dst = (NZ - hop + 1) % NZ, NZ - hop
        else:
            src, dst = hop - 1, hop
        source = w_h.at[span] if (col == 0 and hop == 1) else wg.at[col, src, span]
        sems = (col, direction, hop - 1, part)
        return remote(
            source, wg.at[col, dst, span], ag_send.at[sems], ag_recv.at[sems], ring[direction]
        )

    def reduce_copy(direction, step, part):
        span = (direction, step, slice(None), pl.ds(part * half, half))
        return remote(
            rs_out.at[span], rs_in.at[span],
            rs_send.at[direction, step, part], rs_recv.at[direction, step, part],
            ring[direction],
        )

    for direction in range(2):
        for hop in range(1, HOPS + 1):
            for col in range(2):
                for part in range(2):
                    if hop < HOPS or part == direction:
                        token = ("ag", col, direction, hop, part)
                        copies[token] = gather(*token[1:])
        for step in range(HOPS):
            for part in range(2):
                if step > 0 or part == direction:
                    copies["rs", direction, step, part] = reduce_copy(direction, step, part)

    def exchange(phase, part):
        out = []
        for k in range(1, n_rep):
            peer = lax.rem(rep + k, n_rep)
            src = (stepped, outbox)[phase].at[part, peer]
            dst = final.at[part, rep] if phase else inbox[part].at[rep]
            out.append(
                remote(
                    src, dst,
                    ex_send.at[phase, part, k], ex_recv.at[phase, part, k], (peer, me),
                )
            )
        return out

    ex = {(phase, part): exchange(phase, part) for phase in range(2) for part in range(2)}

    def arrived(key):
        if key not in waited:
            waited.add(key)
            copies[key].wait_recv()

    def block_arrived(col, slot, parts=(0, 1)):
        for part in parts:
            if slot == 0:
                if col == 1:
                    arrived(("wxB",))
            elif slot == HOPS:
                arrived(("ag", col, part, HOPS, part))
            elif slot > HOPS:
                arrived(("ag", col, 0, NZ - slot, part))
            else:
                arrived(("ag", col, 1, slot, part))

    used = []

    def use_block(col, slot):
        block_arrived(col, slot)
        if col == 0 and slot == 0:
            loaded("w")
        loaded("cot")
        loaded((col, slot))
        if col == 0:
            tokens, block = acat[slot, pl.ds(0, tok)], wg[0, slot]
        else:
            tokens, block = aoth[slot, :, low_rows], wg[1, slot, low_rows]
        term = jnp.dot(tokens, block, preferred_element_type=F32)
        if used:
            kvacc[...] += term
        else:
            kvacc[...] = term
        used.append((col, slot))
        back = back_product(ccat[pl.ds(0, tok)], block)
        if col == 0:
            xga[slot] = back
        else:
            xgb[slot, :, low_rows] = back

    sided = []

    def side_products(slot):
        block_arrived(0, slot, (1,))
        arrived(("xs", "cot"))
        arrived(("xs", slot))
        if slot == 0:
            loaded("w")
        block = wg[0, slot, high_rows]
        px_out[slot] = back_product(ccat[pl.ds(tok, tok)], block)
        copies["px", slot].start()
        term = jnp.dot(acat[slot, pl.ds(tok, tok), high_rows], block, preferred_element_type=F32)
        if sided:
            pk_acc[...] += term
        else:
            pk_acc[...] = term
        sided.append(slot)

    def side_sum(part):
        span = pl.ds(part * half, half)
        pk_out[:, span] = pk_acc[:, span].astype(BF)
        copies["pk", part].start()

    def product(slot):
        arrived(("xs", "cot"))
        arrived(("xs", slot))
        loaded("cot")
        loaded((0, slot))
        gbuf[slot] = lax.dot_general(
            acat[slot], ccat[...], (((0,), (0,)), ((), ())), preferred_element_type=F32
        )

    def reduce_send(direction, step, part):
        span = pl.ds(part * half, half)
        slot = HOPS - step if direction == 0 else HOPS + step
        value = gbuf[slot, :, span]
        if ("rs", direction, step - 1, part) in copies:
            arrived(("rs", direction, step - 1, part))
            value = value + rs_in[direction, step - 1, :, span].astype(F32)
        rs_out[direction, step, :, span] = value.astype(BF)
        copies["rs", direction, step, part].start()

    def finish(part):
        span = pl.ds(part * half, half)
        for name in ("first", "second", "w"):
            loaded(name)
        grad = gbuf[0, :, span]
        for direction in range(2):
            arrived(("rs", direction, HOPS - 1, part))
            grad = grad + rs_in[direction, HOPS - 1, :, span].astype(F32)
        new_a = beta_one * mom[0, :, span] + (1.0 - beta_one) * grad
        new_b = beta_two * mom[1, :, span] + (1.0 - beta_two) * grad * grad
        first_new[:, span] = new_a
        second_new[:, span] = new_b
        old = wg[0, 0, :, span].astype(F32)
        update = new_a / corr_one / (jnp.sqrt(new_b / corr_two) + adam_eps) + weight_decay * old
        stepped[part] = (old - learn_rate * update).astype(BF).reshape(stepped.shape[1:])

    def exchange_first(part):
        for copy in ex[0, part]:
            copy.start()
        inbox[part][rep] = stepped[part, rep]

    def exchange_second(part):
        loaded("partner")
        for copy in ex[0, part]:
            copy.wait_recv()
        for j in range(n_rep):
            outbox[part, j] = inbox[part][partner_s[j]]
        for copy in ex[1, part]:
            copy.start()
        final[part, rep] = outbox[part, rep]

    def average():
        loaded("mix")
        mixing = mix_s[rep].astype(F32) / mix_denom
        for part in range(2):
            for copy in ex[1, part]:
                copy.wait_recv()
            own, other = stepped[part].astype(F32), final[part].astype(F32)
            nwv[:, pl.ds(part * half, half)] = (
                ((1.0 - mixing) * own + mixing * other).astype(BF).reshape(rows, half)
            )

    barrier = pltpu.get_barrier_semaphore()
    others = [(lax.rem(rep + k, n_rep), me) for k in range(1, n_rep)]
    for device in (up, down, side, *others):
        pl.semaphore_signal(barrier, inc=1, device_id=device, device_id_type=MESH)
    loads["cot"].start()
    loads["w"].start()
    sends = [token[1] for token in SCHEDULE if token[0] == "xs" and token[1] != "cot"]
    for slot in sends:
        loads[1, slot].start()
    for slot in sends:
        loads[0, slot].start()
    pl.semaphore_wait(barrier, 3 + n_rep - 1)

    actions = {
        "use": use_block, "g": product, "rs": reduce_send, "fin": finish,
        "ex0": exchange_first, "ex1": exchange_second, "px": side_products, "pk": side_sum, "exf": average,
    }
    for position, token in enumerate(SCHEDULE):
        if position == LATE_LOADS:
            for name in ("first", "second", "partner", "mix"):
                loads[name].start()
        name = token[0]
        if name in actions:
            actions[name](*token[1:])
            continue
        if name == "ag":
            _, col, direction, hop, part = token
            if hop > 1:
                arrived(("ag", col, direction, hop - 1, part))
            elif col == 1:
                arrived(("wxB",))
        elif name == "xs" and token[1] != "cot":
            loaded((1, token[1]))
        copies[token].start()

    for key in loads:
        loaded(key)
    for phase in range(2):
        for part in range(2):
            for copy in ex[phase, part]:
                copy.wait_send()
    sent = [token for token in SCHEDULE if token in copies]
    for token in sent[:-LAST]:
        copies[token].wait_send()
    for token in sent:
        arrived(token)
    for token in sent[-LAST:]:
        copies[token].wait_send()


LAST = 8
LATE_LOADS = 17
LEFT = tuple(
    (col, slot)
    for slot in (0, 7, 1, 6, 2, 5, 3, 4)
    for col in range(2)
    if ("use", col, slot) not in SCHEDULE
)


def write_out(
    kvacc, xga, xgb, kvc, first_new, second_new, nwv, wg, aoth, ccat,
    kv_h, xg_h, nw_h, nf_h, ns_h,
    kvb, xgl, xg_sem, sem,
):
    tok = kvb.shape[0]
    rows = nwv.shape[0]
    copies = [
        pltpu.make_async_copy(first_new, nf_h, sem.at[0]),
        pltpu.make_async_copy(second_new, ns_h, sem.at[1]),
        pltpu.make_async_copy(nwv, nw_h, sem.at[3]),
    ]
    for slot in range(NZ):
        blocks = [(xga.at[slot], 0, None)]
        if (1, slot) in LEFT:
            blocks.append((xgb.at[slot, :, pl.ds(rows // 2, rows // 2)], 1, 1))
        else:
            blocks.append((xgb.at[slot], 1, None))
        for source, col, part in blocks:
            copies.append(
                pltpu.make_async_copy(
                    source, columns_of(xg_h, col, slot, rows, part), xg_sem.at[col, slot]
                )
            )
    for copy in copies:
        copy.start()
    total = kvacc[...] + kvc[...].astype(F32)
    for i, (col, slot) in enumerate(LEFT):
        block = wg[col, slot, pl.ds(0, rows // 2)]
        total = total + jnp.dot(aoth[slot, :, pl.ds(0, rows // 2)], block, preferred_element_type=F32)
        xgl[i] = back_product(ccat[pl.ds(0, tok)], block)
        copy = pltpu.make_async_copy(
            xgl.at[i], columns_of(xg_h, col, slot, rows, 0), xg_sem.at[2, slot]
        )
        copy.start()
        copies.append(copy)
    kvb[...] = total.astype(BF)
    copies.append(pltpu.make_async_copy(kvb, kv_h, sem.at[2]))
    copies[-1].start()
    for copy in copies:
        copy.wait()


def per_device(
    activations, kv_weight, kv_cotangent, first_moment, second_moment, partner, mix_numerator
):
    act, weights, cot = activations[0], kv_weight[0], kv_cotangent[0]
    tok, width = act.shape
    rows, cols = weights.shape
    n_rep = partner.shape[0]
    chunks = (2, n_rep, rows // n_rep, cols // 2)
    dma = pltpu.SemaphoreType.DMA
    hbm = pl.BlockSpec(memory_space=pltpu.HBM)
    vmem = pl.BlockSpec(memory_space=pltpu.VMEM)

    def in_hbm(x):
        return pltpu.with_memory_space_constraint(x, pltpu.HBM)

    held = pl.pallas_call(
        kernel,
        out_shape=(
            pltpu.VMEM((tok, cols), F32),
            pltpu.VMEM((NZ, tok, rows), BF),
            pltpu.VMEM((NZ, tok, rows), BF),
            pltpu.VMEM((tok, cols), BF),
            pltpu.VMEM((rows, cols), F32),
            pltpu.VMEM((rows, cols), F32),
            pltpu.VMEM((rows, cols), BF),
            pltpu.VMEM((2, NZ, rows, cols), BF),
            pltpu.VMEM((NZ, tok, rows), BF),
            pltpu.VMEM((2 * tok, cols), BF),
        ),
        in_specs=[hbm] * 7,
        out_specs=[vmem] * 10,
        scratch_shapes=[
            pltpu.VMEM(chunks, BF),
            pltpu.VMEM(chunks, BF),
            pltpu.VMEM((NZ, tok, rows // 2), BF),
            pltpu.VMEM((tok, cols), BF),
            pltpu.VMEM((tok, cols), F32),
            pltpu.VMEM((NZ, 2 * tok, rows), BF),
            pltpu.VMEM((2, rows, cols), F32),
            pltpu.VMEM((2, HOPS, rows, cols), BF),
            pltpu.VMEM((2, HOPS, rows, cols), BF),
            pltpu.VMEM((NZ, rows, cols), F32),
            pltpu.VMEM(chunks[1:], BF),
            pltpu.VMEM(chunks[1:], BF),
            pltpu.VMEM(chunks, BF),
            pltpu.SMEM((n_rep,), jnp.int32),
            pltpu.SMEM((n_rep,), jnp.int32),
            dma((6,)),
            dma((2, NZ)),
            dma((NZ + 1,)),
            dma((NZ + 1,)),
            dma((1,)),
            dma((1,)),
            dma((2, 2, HOPS, 2)),
            dma((2, 2, HOPS, 2)),
            dma((2, HOPS, 2)),
            dma((2, HOPS, 2)),
            dma((2, 2, n_rep)),
            dma((2, 2, n_rep)),
            dma((NZ,)),
            dma((NZ,)),
            dma((2,)),
            dma((2,)),
        ],
        name="step",
        compiler_params=pltpu.CompilerParams(
            collective_id=0, has_side_effects=True, vmem_limit_bytes=32 << 20
        ),
    )(
        *(
            in_hbm(x)
            for x in (act, weights, cot, first_moment[0], second_moment[0], partner, mix_numerator)
        )
    )
    outs = pl.pallas_call(
        write_out,
        out_shape=(
            jax.ShapeDtypeStruct((tok, cols), BF),
            jax.ShapeDtypeStruct((tok, width), BF),
            jax.ShapeDtypeStruct((rows, cols), BF),
            jax.ShapeDtypeStruct((rows, cols), F32),
            jax.ShapeDtypeStruct((rows, cols), F32),
        ),
        in_specs=[vmem] * 10,
        out_specs=[hbm] * 5,
        scratch_shapes=[
            pltpu.VMEM((tok, cols), BF),
            pltpu.VMEM((len(LEFT), tok, rows // 2), BF),
            dma((3, NZ)),
            dma((4,)),
        ],
        name="write_out",
        compiler_params=pltpu.CompilerParams(vmem_limit_bytes=8 << 20),
    )(*held)
    return tuple(out[None] for out in outs)


def solution(mesh):
    split = P("rep", "fsdp", None)
    return jax.shard_map(
        per_device,
        mesh=mesh,
        in_specs=(split,) * 5 + (P(), P()),
        out_specs=(split,) * 5,
        check_vma=False,
    )
```

```python
import jax
import jax.numpy as jnp
from jax import lax
from jax.experimental import pallas as pl
from jax.experimental.pallas import tpu as pltpu
from jax.sharding import PartitionSpec as P

beta_one = 0.9
beta_two = 0.999
learn_rate = 0.02
weight_decay = 0.1
adam_eps = 1e-08
corr_one = 1.0 - beta_one**10
corr_two = 1.0 - beta_two**10
mix_denom = 64.0

MESH = pl.DeviceIdType.MESH
BF = jnp.bfloat16
F32 = jnp.float32
NZ = 8
HOPS = NZ // 2

SCHEDULE = (
    ("xs", "cot"), ("ag", 0, 1, 1, 0), ("ag", 0, 0, 1, 1), ("ag", 0, 0, 1, 0),
    ("ag", 0, 1, 1, 1), ("xs", 4), ("xs", 3), ("xs", 5), ("ag", 0, 0, 2, 1), ("xs", 2),
    ("xs", 1), ("xs", 6), ("ag", 0, 1, 2, 0), ("ag", 0, 1, 2, 1), ("ag", 0, 0, 2, 0), ("xs", 0),
    ("ag", 0, 0, 3, 1), ("g", 4), ("rs", 1, 0, 1), ("ag", 0, 1, 3, 1), ("rs", 0, 0, 0), ("g", 5),
    ("xs", 7), ("rs", 1, 1, 1), ("wxB",), ("g", 3), ("rs", 0, 1, 1), ("use", 0, 7),
    ("rs", 1, 1, 0), ("rs", 0, 1, 0), ("use", 0, 0), ("g", 2), ("g", 1), ("g", 6),
    ("rs", 0, 2, 1), ("rs", 1, 2, 1), ("px", 6), ("px", 5), ("rs", 1, 2, 0), ("rs", 0, 2, 0),
    ("g", 7), ("g", 0), ("rs", 0, 3, 1), ("px", 2), ("rs", 1, 3, 1), ("use", 0, 6),
    ("rs", 1, 3, 0), ("px", 0), ("rs", 0, 3, 0), ("ag", 1, 0, 1, 1), ("ag", 1, 0, 1, 0),
    ("px", 7), ("px", 1), ("use", 1, 0), ("fin", 1), ("ex0", 1), ("ag", 0, 1, 4, 1),
    ("ag", 0, 0, 3, 0), ("px", 3), ("ag", 1, 1, 1, 1), ("fin", 0), ("ex0", 0), ("use", 0, 2),
    ("ag", 1, 0, 2, 1), ("ag", 1, 1, 1, 0), ("ag", 0, 1, 3, 0), ("ex1", 1), ("use", 1, 7),
    ("ag", 1, 0, 2, 0), ("px", 4), ("pk", 0), ("ex1", 0), ("ag", 1, 1, 2, 1), ("pk", 1),
    ("ag", 1, 0, 3, 1), ("ag", 1, 0, 3, 0), ("ag", 1, 1, 2, 0), ("ag", 0, 0, 4, 0),
    ("use", 1, 6), ("ag", 1, 1, 3, 1), ("use", 0, 3), ("ag", 1, 1, 3, 0), ("use", 0, 5),
    ("use", 1, 1), ("use", 0, 1), ("ag", 1, 1, 4, 1), ("ag", 1, 0, 4, 0), ("use", 1, 2),
    ("exf",), ("use", 1, 5), ("use", 0, 4), ("use", 1, 3),
)


def column_index(col, slot):
    me = lax.axis_index("fsdp")
    x = me % 2
    return lax.rem(me // 2 + slot, NZ) * 2 + (x if col == 0 else 1 - x)


def columns_of(ref, col, slot, rows, part=None):
    start = column_index(col, slot) * rows
    if part is not None:
        rows = rows // 2
        start = start + part * rows
    return ref.at[:, pl.ds(pl.multiple_of(start, rows), rows)]


def back_product(cot, block):
    return lax.dot_general(
        cot, block, (((1,), (1,)), ((), ())), preferred_element_type=F32
    ).astype(BF)


def kernel(
    act_h, w_h, cot_h, first_h, second_h, partner_h, mix_h,
    kvacc, xga, xgb, kvc, first_new, second_new, nwv, wg, aoth, ccat,
    stepped, final, px_out, pk_out, pk_acc, acat, mom, rs_in, rs_out, gbuf, inbox_a, inbox_b, outbox, partner_s, mix_s,
    load_sem, act_sem, x_send, x_recv, wx_send, wx_recv, ag_send, ag_recv,
    rs_send, rs_recv, ex_send, ex_recv, px_send, px_recv, pk_send, pk_recv,
):
    rep = lax.axis_index("rep")
    me = lax.axis_index("fsdp")
    inbox = (inbox_a, inbox_b)
    n_rep = inbox_a.shape[0]
    tok = cot_h.shape[0]
    rows, cols = w_h.shape
    half = cols // 2
    low_rows, high_rows = pl.ds(0, rows // 2), pl.ds(rows // 2, rows // 2)
    z, xl = me // 2, me % 2
    up = (rep, lax.rem(z + 1, NZ) * 2 + xl)
    down = (rep, lax.rem(z + NZ - 1, NZ) * 2 + xl)
    side = (rep, z * 2 + 1 - xl)
    ring = (up, down)

    def remote(src, dst, send, recv, target):
        return pltpu.make_async_remote_copy(
            src_ref=src, dst_ref=dst, send_sem=send, recv_sem=recv,
            device_id=target, device_id_type=MESH,
        )

    loads = {
        "cot": pltpu.make_async_copy(cot_h, ccat.at[pl.ds(0, tok)], load_sem.at[0]),
        "w": pltpu.make_async_copy(w_h, wg.at[0, 0], load_sem.at[1]),
        "first": pltpu.make_async_copy(first_h, mom.at[0], load_sem.at[2]),
        "second": pltpu.make_async_copy(second_h, mom.at[1], load_sem.at[3]),
        "partner": pltpu.make_async_copy(partner_h, partner_s, load_sem.at[4]),
        "mix": pltpu.make_async_copy(mix_h, mix_s, load_sem.at[5]),
    }
    for slot in range(NZ):
        loads[0, slot] = pltpu.make_async_copy(
            columns_of(act_h, 0, slot, rows), acat.at[slot, pl.ds(0, tok)], act_sem.at[0, slot]
        )
        loads[1, slot] = pltpu.make_async_copy(
            columns_of(act_h, 1, slot, rows), aoth.at[slot], act_sem.at[1, slot]
        )
    waited = set()

    def loaded(key):
        if key not in waited:
            waited.add(key)
            loads[key].wait()

    copies = {
        ("xs", "cot"): remote(
            cot_h, ccat.at[pl.ds(tok, tok)], x_send.at[NZ], x_recv.at[NZ], side
        ),
        ("wxB",): remote(
            w_h.at[low_rows], wg.at[1, 0, low_rows], wx_send.at[0], wx_recv.at[0], side
        ),
    }
    for slot in range(NZ):
        copies["xs", slot] = remote(
            aoth.at[slot], acat.at[slot, pl.ds(tok, tok)],
            x_send.at[slot], x_recv.at[slot], side,
        )
        copies["px", slot] = remote(
            px_out.at[slot], xgb.at[slot, :, high_rows], px_send.at[slot], px_recv.at[slot], side
        )
    for part in range(2):
        span = (slice(None), pl.ds(part * half, half))
        copies["pk", part] = remote(
            pk_out.at[span], kvc.at[span], pk_send.at[part], pk_recv.at[part], side
        )

    def gather(col, direction, hop, part):
        length = rows // 2 if col == 0 else rows // 4
        span = pl.ds(part * length, length)
        if direction == 0:
            src, dst = (NZ - hop + 1) % NZ, NZ - hop
        else:
            src, dst = hop - 1, hop
        source = w_h.at[span] if (col == 0 and hop == 1) else wg.at[col, src, span]
        sems = (col, direction, hop - 1, part)
        return remote(
            source, wg.at[col, dst, span], ag_send.at[sems], ag_recv.at[sems], ring[direction]
        )

    def reduce_copy(direction, step, part):
        span = (direction, step, slice(None), pl.ds(part * half, half))
        return remote(
            rs_out.at[span], rs_in.at[span],
            rs_send.at[direction, step, part], rs_recv.at[direction, step, part],
            ring[direction],
        )

    for direction in range(2):
        for hop in range(1, HOPS + 1):
            for col in range(2):
                for part in range(2):
                    if hop < HOPS or part == direction:
                        token = ("ag", col, direction, hop, part)
                        copies[token] = gather(*token[1:])
        for step in range(HOPS):
            for part in range(2):
                if step > 0 or part == direction:
                    copies["rs", direction, step, part] = reduce_copy(direction, step, part)

    def exchange(phase, part):
        out = []
        for k in range(1, n_rep):
            peer = lax.rem(rep + k, n_rep)
            src = (stepped, outbox)[phase].at[part, peer]
            dst = final.at[part, rep] if phase else inbox[part].at[rep]
            out.append(
                remote(
                    src, dst,
                    ex_send.at[phase, part, k], ex_recv.at[phase, part, k], (peer, me),
                )
            )
        return out

    ex = {(phase, part): exchange(phase, part) for phase in range(2) for part in range(2)}

    def arrived(key):
        if key not in waited:
            waited.add(key)
            copies[key].wait_recv()

    def block_arrived(col, slot, parts=(0, 1)):
        for part in parts:
            if slot == 0:
                if col == 1:
                    arrived(("wxB",))
            elif slot == HOPS:
                arrived(("ag", col, part, HOPS, part))
            elif slot > HOPS:
                arrived(("ag", col, 0, NZ - slot, part))
            else:
                arrived(("ag", col, 1, slot, part))

    used = []

    def use_block(col, slot):
        block_arrived(col, slot)
        if col == 0 and slot == 0:
            loaded("w")
        loaded("cot")
        loaded((col, slot))
        if col == 0:
            tokens, block = acat[slot, pl.ds(0, tok)], wg[0, slot]
        else:
            tokens, block = aoth[slot, :, low_rows], wg[1, slot, low_rows]
        term = jnp.dot(tokens, block, preferred_element_type=F32)
        if used:
            kvacc[...] += term
        else:
            kvacc[...] = term
        used.append((col, slot))
        back = back_product(ccat[pl.ds(0, tok)], block)
        if col == 0:
            xga[slot] = back
        else:
            xgb[slot, :, low_rows] = back

    sided = []

    def side_products(slot):
        block_arrived(0, slot, (1,))
        arrived(("xs", "cot"))
        arrived(("xs", slot))
        if slot == 0:
            loaded("w")
        block = wg[0, slot, high_rows]
        px_out[slot] = back_product(ccat[pl.ds(tok, tok)], block)
        copies["px", slot].start()
        term = jnp.dot(acat[slot, pl.ds(tok, tok), high_rows], block, preferred_element_type=F32)
        if sided:
            pk_acc[...] += term
        else:
            pk_acc[...] = term
        sided.append(slot)

    def side_sum(part):
        span = pl.ds(part * half, half)
        pk_out[:, span] = pk_acc[:, span].astype(BF)
        copies["pk", part].start()

    def product(slot):
        arrived(("xs", "cot"))
        arrived(("xs", slot))
        loaded("cot")
        loaded((0, slot))
        gbuf[slot] = lax.dot_general(
            acat[slot], ccat[...], (((0,), (0,)), ((), ())), preferred_element_type=F32
        )

    def reduce_send(direction, step, part):
        span = pl.ds(part * half, half)
        slot = HOPS - step if direction == 0 else HOPS + step
        value = gbuf[slot, :, span]
        if ("rs", direction, step - 1, part) in copies:
            arrived(("rs", direction, step - 1, part))
            value = value + rs_in[direction, step - 1, :, span].astype(F32)
        rs_out[direction, step, :, span] = value.astype(BF)
        copies["rs", direction, step, part].start()

    def finish(part):
        span = pl.ds(part * half, half)
        for name in ("first", "second", "w"):
            loaded(name)
        grad = gbuf[0, :, span]
        for direction in range(2):
            arrived(("rs", direction, HOPS - 1, part))
            grad = grad + rs_in[direction, HOPS - 1, :, span].astype(F32)
        new_a = beta_one * mom[0, :, span] + (1.0 - beta_one) * grad
        new_b = beta_two * mom[1, :, span] + (1.0 - beta_two) * grad * grad
        first_new[:, span] = new_a
        second_new[:, span] = new_b
        old = wg[0, 0, :, span].astype(F32)
        update = new_a / corr_one / (jnp.sqrt(new_b / corr_two) + adam_eps) + weight_decay * old
        stepped[part] = (old - learn_rate * update).astype(BF).reshape(stepped.shape[1:])

    def exchange_first(part):
        for copy in ex[0, part]:
            copy.start()
        inbox[part][rep] = stepped[part, rep]

    def exchange_second(part):
        loaded("partner")
        for copy in ex[0, part]:
            copy.wait_recv()
        for j in range(n_rep):
            outbox[part, j] = inbox[part][partner_s[j]]
        for copy in ex[1, part]:
            copy.start()
        final[part, rep] = outbox[part, rep]

    def average():
        loaded("mix")
        mixing = mix_s[rep].astype(F32) / mix_denom
        for part in range(2):
            for copy in ex[1, part]:
                copy.wait_recv()
            own, other = stepped[part].astype(F32), final[part].astype(F32)
            nwv[:, pl.ds(part * half, half)] = (
                ((1.0 - mixing) * own + mixing * other).astype(BF).reshape(rows, half)
            )

    barrier = pltpu.get_barrier_semaphore()
    others = [(lax.rem(rep + k, n_rep), me) for k in range(1, n_rep)]
    for device in (up, down, side, *others):
        pl.semaphore_signal(barrier, inc=1, device_id=device, device_id_type=MESH)
    sends = [token[1] for token in SCHEDULE if token[0] == "xs" and token[1] != "cot"]
    pl.semaphore_wait(barrier, 3 + n_rep - 1)

    actions = {
        "use": use_block, "g": product, "rs": reduce_send, "fin": finish,
        "ex0": exchange_first, "ex1": exchange_second, "px": side_products, "pk": side_sum, "exf": average,
    }
    for position, token in enumerate(SCHEDULE):
        if position == FIRST_LOADS:
            for slot in sends:
                loads[1, slot].start()
            for key in ("cot", "w", *((0, slot) for slot in sends)):
                loads[key].start()
        if position == LATE_LOADS:
            for name in ("first", "second", "partner", "mix"):
                loads[name].start()
        name = token[0]
        if name in actions:
            actions[name](*token[1:])
            continue
        if name == "ag":
            _, col, direction, hop, part = token
            if hop > 1:
                arrived(("ag", col, direction, hop - 1, part))
            elif col == 1:
                arrived(("wxB",))
        elif name == "xs" and token[1] != "cot":
            loaded((1, token[1]))
        copies[token].start()

    for key in loads:
        loaded(key)
    for phase in range(2):
        for part in range(2):
            for copy in ex[phase, part]:
                copy.wait_send()
    sent = [token for token in SCHEDULE if token in copies]
    for token in sent[:-LAST]:
        copies[token].wait_send()
    for token in sent:
        arrived(token)
    for token in sent[-LAST:]:
        copies[token].wait_send()


LAST = 8
FIRST_LOADS = 5
LATE_LOADS = 17
LEFT = tuple(
    (col, slot)
    for slot in (0, 7, 1, 6, 2, 5, 3, 4)
    for col in range(2)
    if ("use", col, slot) not in SCHEDULE
)


def write_out(
    kvacc, xga, xgb, kvc, first_new, second_new, nwv, wg, aoth, ccat,
    kv_h, xg_h, nw_h, nf_h, ns_h,
    kvb, xgl, xg_sem, sem,
):
    tok = kvb.shape[0]
    rows = nwv.shape[0]
    copies = [
        pltpu.make_async_copy(first_new, nf_h, sem.at[0]),
        pltpu.make_async_copy(second_new, ns_h, sem.at[1]),
        pltpu.make_async_copy(nwv, nw_h, sem.at[3]),
    ]
    for slot in range(NZ):
        blocks = [(xga.at[slot], 0, None)]
        if (1, slot) in LEFT:
            blocks.append((xgb.at[slot, :, pl.ds(rows // 2, rows // 2)], 1, 1))
        else:
            blocks.append((xgb.at[slot], 1, None))
        for source, col, part in blocks:
            copies.append(
                pltpu.make_async_copy(
                    source, columns_of(xg_h, col, slot, rows, part), xg_sem.at[col, slot]
                )
            )
    for copy in copies:
        copy.start()
    total = kvacc[...] + kvc[...].astype(F32)
    for i, (col, slot) in enumerate(LEFT):
        block = wg[col, slot, pl.ds(0, rows // 2)]
        total = total + jnp.dot(aoth[slot, :, pl.ds(0, rows // 2)], block, preferred_element_type=F32)
        xgl[i] = back_product(ccat[pl.ds(0, tok)], block)
        copy = pltpu.make_async_copy(
            xgl.at[i], columns_of(xg_h, col, slot, rows, 0), xg_sem.at[2, slot]
        )
        copy.start()
        copies.append(copy)
    kvb[...] = total.astype(BF)
    copies.append(pltpu.make_async_copy(kvb, kv_h, sem.at[2]))
    copies[-1].start()
    for copy in copies:
        copy.wait()


def per_device(
    activations, kv_weight, kv_cotangent, first_moment, second_moment, partner, mix_numerator
):
    act, weights, cot = activations[0], kv_weight[0], kv_cotangent[0]
    tok, width = act.shape
    rows, cols = weights.shape
    n_rep = partner.shape[0]
    chunks = (2, n_rep, rows // n_rep, cols // 2)
    dma = pltpu.SemaphoreType.DMA
    hbm = pl.BlockSpec(memory_space=pltpu.HBM)
    vmem = pl.BlockSpec(memory_space=pltpu.VMEM)

    def in_hbm(x):
        return pltpu.with_memory_space_constraint(x, pltpu.HBM)

    held = pl.pallas_call(
        kernel,
        out_shape=(
            pltpu.VMEM((tok, cols), F32),
            pltpu.VMEM((NZ, tok, rows), BF),
            pltpu.VMEM((NZ, tok, rows), BF),
            pltpu.VMEM((tok, cols), BF),
            pltpu.VMEM((rows, cols), F32),
            pltpu.VMEM((rows, cols), F32),
            pltpu.VMEM((rows, cols), BF),
            pltpu.VMEM((2, NZ, rows, cols), BF),
            pltpu.VMEM((NZ, tok, rows), BF),
            pltpu.VMEM((2 * tok, cols), BF),
        ),
        in_specs=[hbm] * 7,
        out_specs=[vmem] * 10,
        scratch_shapes=[
            pltpu.VMEM(chunks, BF),
            pltpu.VMEM(chunks, BF),
            pltpu.VMEM((NZ, tok, rows // 2), BF),
            pltpu.VMEM((tok, cols), BF),
            pltpu.VMEM((tok, cols), F32),
            pltpu.VMEM((NZ, 2 * tok, rows), BF),
            pltpu.VMEM((2, rows, cols), F32),
            pltpu.VMEM((2, HOPS, rows, cols), BF),
            pltpu.VMEM((2, HOPS, rows, cols), BF),
            pltpu.VMEM((NZ, rows, cols), F32),
            pltpu.VMEM(chunks[1:], BF),
            pltpu.VMEM(chunks[1:], BF),
            pltpu.VMEM(chunks, BF),
            pltpu.SMEM((n_rep,), jnp.int32),
            pltpu.SMEM((n_rep,), jnp.int32),
            dma((6,)),
            dma((2, NZ)),
            dma((NZ + 1,)),
            dma((NZ + 1,)),
            dma((1,)),
            dma((1,)),
            dma((2, 2, HOPS, 2)),
            dma((2, 2, HOPS, 2)),
            dma((2, HOPS, 2)),
            dma((2, HOPS, 2)),
            dma((2, 2, n_rep)),
            dma((2, 2, n_rep)),
            dma((NZ,)),
            dma((NZ,)),
            dma((2,)),
            dma((2,)),
        ],
        name="step",
        compiler_params=pltpu.CompilerParams(
            collective_id=0, has_side_effects=True, vmem_limit_bytes=32 << 20
        ),
    )(
        *(
            in_hbm(x)
            for x in (act, weights, cot, first_moment[0], second_moment[0], partner, mix_numerator)
        )
    )
    outs = pl.pallas_call(
        write_out,
        out_shape=(
            jax.ShapeDtypeStruct((tok, cols), BF),
            jax.ShapeDtypeStruct((tok, width), BF),
            jax.ShapeDtypeStruct((rows, cols), BF),
            jax.ShapeDtypeStruct((rows, cols), F32),
            jax.ShapeDtypeStruct((rows, cols), F32),
        ),
        in_specs=[vmem] * 10,
        out_specs=[hbm] * 5,
        scratch_shapes=[
            pltpu.VMEM((tok, cols), BF),
            pltpu.VMEM((len(LEFT), tok, rows // 2), BF),
            dma((3, NZ)),
            dma((4,)),
        ],
        name="write_out",
        compiler_params=pltpu.CompilerParams(vmem_limit_bytes=8 << 20),
    )(*held)
    return tuple(out[None] for out in outs)


def solution(mesh):
    split = P("rep", "fsdp", None)
    return jax.shard_map(
        per_device,
        mesh=mesh,
        in_specs=(split,) * 5 + (P(), P()),
        out_specs=(split,) * 5,
        check_vma=False,
    )
```
